32 devices in a mesh: dp: 4 (over y, x), tensor: 8 (over z, core).
Axes of the slice: x: 2, y: 2, z: 4, core: 2. Of those that a mesh axis runs over, the one named last changes fastest.
Arguments:
- block_in: bfloat16 [8192, 1024], P(('dp', 'tensor')), may hold values from -10 to 10
- cotangent: bfloat16 [8192, 1024], P(('dp', 'tensor')), may hold values from -6 to 6
- lengths: int32 [16], P('dp'), may hold values from 1 to 512, as said below
- qkv_weight: float32 [3, 1024, 1024], P(None, 'dp', 'tensor'), may hold values from -0.1875 to 0.1875
- proj_weight: float32 [1024, 1024], P('tensor', 'dp'), may hold values from -0.75 to 0.75
- expand_weight: float32 [1024, 4096], P('dp', 'tensor'), may hold values from -0.1875 to 0.1875
- reduce_weight: float32 [4096, 1024], P('tensor', 'dp'), may hold values from -0.09375 to 0.09375
- split_bias: float32 [16, 384], P('tensor', 'dp'), may hold values from -0.6 to 0.6
- vector_params: float32 [6, 1024], P(None, 'dp'), may hold values from -0.6 to 0.6
- qkv_moments: float32 [2, 3, 1024, 1024], P(None, None, 'dp', 'tensor'), may hold values from -3 to 3, as said below
- proj_moments: float32 [2, 1024, 1024], P(None, 'tensor', 'dp'), may hold values from -3 to 3, as said below
- expand_moments: float32 [2, 1024, 4096], P(None, 'dp', 'tensor'), may hold values from -3 to 3, as said below
- reduce_moments: float32 [2, 4096, 1024], P(None, 'tensor', 'dp'), may hold values from -3 to 3, as said below
- bias_moments: float32 [2, 16, 384], P(None, 'tensor', 'dp'), may hold values from -3 to 3, as said below
- vector_moments: float32 [2, 6, 1024], P(None, None, 'dp'), may hold values from -3 to 3, as said below
Outputs:
- block_out: bfloat16 [8192, 1024], P(('dp', 'tensor'))
- input_grad: bfloat16 [8192, 1024], P(('dp', 'tensor'))
- qkv_grad: float32 [3, 1024, 1024], P(None, 'dp', 'tensor')
- proj_grad: float32 [1024, 1024], P('tensor', 'dp')
- expand_grad: float32 [1024, 4096], P('dp', 'tensor')
- reduce_grad: float32 [4096, 1024], P('tensor', 'dp')
- bias_grad: float32 [16, 384], P('tensor', 'dp')
- vector_grad: float32 [6, 1024], P(None, 'dp')
- qkv_new: float32 [3, 1024, 1024], P(None, 'dp', 'tensor')
- proj_new: float32 [1024, 1024], P('tensor', 'dp')
- expand_new: float32 [1024, 4096], P('dp', 'tensor')
- reduce_new: float32 [4096, 1024], P('tensor', 'dp')
- bias_new: float32 [16, 384], P('tensor', 'dp')
- vector_new: float32 [6, 1024], P(None, 'dp')
- qkv_state: float32 [2, 3, 1024, 1024], P(None, None, 'dp', 'tensor')
- proj_state: float32 [2, 1024, 1024], P(None, 'tensor', 'dp')
- expand_state: float32 [2, 1024, 4096], P(None, 'dp', 'tensor')
- reduce_state: float32 [2, 4096, 1024], P(None, 'tensor', 'dp')
- bias_state: float32 [2, 16, 384], P(None, 'tensor', 'dp')
- vector_state: float32 [2, 6, 1024], P(None, None, 'dp')
The draws below stay inside these ranges and needn't reach their ends.
Inputs may be any that keep to these rules, and one draw needn't show every extreme that they name: `lengths`: sequence s lies on the dp member s // (number of sequences per dp member); every draw has a sequence of exactly 512 live slots. `qkv_moments`: index 0 holds first moments, index 1 second moments of at least 0.01. `proj_moments`: index 0 holds first moments, index 1 second moments of at least 0.01. `expand_moments`: index 0 holds first moments, index 1 second moments of at least 0.01. `reduce_moments`: index 0 holds first moments, index 1 second moments of at least 0.01. `bias_moments`: index 0 holds first moments, index 1 second moments of at least 0.01. `vector_moments`: index 0 holds first moments, index 1 second moments of at least 0.01.
All inputs are finite; a program needn't handle non-finite values.
Results may differ from the reference program's by a relative error of at most 0.025.
Values may be sent and summed in bfloat16 or wider, within the bound.
No kernel may reach another device: no remote copies, remote signals or barrier semaphores. Data moves between devices by JAX's collectives and lax.ppermute only.
A program may use at most 192 MiB of HBM per device.

```python
import jax
import jax.numpy as jnp
from jax import lax

D = 1024
H = 16
FF = 4096
L = 512
SEQS_DEV = 4
STEP = 10
HD = 64
TOK_DEV = 2048
SEQS = 16
TOKENS = 8192
BIAS_W = 384
N_DP = 4
N_TENSOR = 8


def moment_pair(key, shape):
    first_key = jax.random.fold_in(key, 11)
    second_key = jax.random.fold_in(key, 12)
    first = 0.5 * jnp.clip(jax.random.normal(first_key, shape, jnp.float32), -6.0, 6.0)
    second = jnp.exp(jax.random.uniform(second_key, shape, jnp.float32, -4.6, 0.0))
    return jnp.stack([first, second])


def draw_qkv_moments(key, part):
    return moment_pair(key, (3, D, D))


def draw_proj_moments(key, part):
    return moment_pair(key, (D, D))


def draw_expand_moments(key, part):
    return moment_pair(key, (D, FF))


def draw_reduce_moments(key, part):
    return moment_pair(key, (FF, D))


def draw_bias_moments(key, part):
    return moment_pair(key, (H, BIAS_W))


def draw_vector_moments(key, part):
    return moment_pair(key, (6, D))


def draw_block_in(key, part):
    base_key = jax.random.fold_in(key, 21)
    values = jnp.clip(jax.random.normal(base_key, (TOKENS, D), jnp.float32), -6.0, 6.0)
    return values.astype(jnp.bfloat16)


def draw_lengths(key, part):
    fill_key = jax.random.fold_in(key, 31)
    size_key = jax.random.fold_in(key, 32)
    slot_key = jax.random.fold_in(key, 33)
    quarters = jax.random.randint(fill_key, (SEQS // SEQS_DEV, 1), 1, 5)
    upper = quarters * L // 4
    lower = jnp.maximum(upper // 2, 1)
    raw = jax.random.randint(size_key, (SEQS // SEQS_DEV, SEQS_DEV), 0, 1 << 20)
    sized = (lower + raw % (upper - lower + 1)).reshape(-1)
    full_slot = jax.random.randint(slot_key, (), 0, SEQS)
    return jnp.where(jnp.arange(SEQS) == full_slot, L, sized).astype(jnp.int32)


def steps_of(own_key, shape, split, low, largest):
    factor_of, own = 1.0, jax.random.fold_in(own_key, 6)
    for dim, parts in split:
        draws = jnp.exp(jax.random.uniform(jax.random.fold_in(own, dim), (parts,), jnp.float32, low / len(split), largest / len(split)))
        factor_of = factor_of * jnp.repeat(draws, shape[dim] // parts).reshape([-1 if axis == dim else 1 for axis in range(len(shape))])
    return factor_of


def centred(rng, dims, deviation, most, cuts=(), kind=jnp.bfloat16):
    level = steps_of(rng, dims, cuts, -0.22, 0.18) if cuts else 1.0
    entries = jax.random.normal(rng, dims, jnp.float32) * deviation * level
    return jnp.minimum(jnp.maximum(entries, -most), most).astype(kind)


def setup_inputs(seed: int = 0) -> dict:
    key_list = jax.random.split(jax.random.key(seed), 16)
    block_in = draw_block_in(jax.random.fold_in(key_list[15], 71), 0)
    cotangent = centred(key_list[1], (TOKENS, D), 1.0, 6.0, ((0, 32),))
    lengths = draw_lengths(jax.random.fold_in(key_list[15], 71), 0)
    qkv_weight = centred(key_list[3], (3, D, D), D ** -0.5, 0.1875, ((1, 4), (2, 8)), jnp.float32)
    proj_weight = centred(key_list[4], (D, D), (max(D // 16, 1)) ** -0.5, 0.75, ((0, 8), (1, 4)), jnp.float32)
    expand_weight = centred(key_list[5], (D, FF), D ** -0.5, 0.1875, ((0, 4), (1, 8)), jnp.float32)
    reduce_weight = centred(key_list[6], (FF, D), FF ** -0.5, 0.09375, ((0, 8), (1, 4)), jnp.float32)
    split_bias = centred(key_list[7], (H, BIAS_W), 0.1, 0.6, ((0, 8), (1, 4)), jnp.float32)
    vector_params = centred(key_list[8], (6, D), 0.1, 0.6, ((1, 4),), jnp.float32)
    qkv_moments = draw_qkv_moments(jax.random.fold_in(key_list[15], 71), 0)
    proj_moments = draw_proj_moments(jax.random.fold_in(key_list[15], 71), 0)
    expand_moments = draw_expand_moments(jax.random.fold_in(key_list[15], 71), 0)
    reduce_moments = draw_reduce_moments(jax.random.fold_in(key_list[15], 71), 0)
    bias_moments = draw_bias_moments(jax.random.fold_in(key_list[15], 71), 0)
    vector_moments = draw_vector_moments(jax.random.fold_in(key_list[15], 71), 0)
    return dict(block_in=block_in, cotangent=cotangent, lengths=lengths, qkv_weight=qkv_weight, proj_weight=proj_weight, expand_weight=expand_weight, reduce_weight=reduce_weight, split_bias=split_bias, vector_params=vector_params, qkv_moments=qkv_moments, proj_moments=proj_moments, expand_moments=expand_moments, reduce_moments=reduce_moments, bias_moments=bias_moments, vector_moments=vector_moments)


norm_eps = 1e-05
beta_one = 0.9
beta_two = 0.999
learn_rate = 0.02
decay_rate = 0.01
adam_eps = 1e-08

def layer_norm(resid, gain, shift):
    center = resid - lax.optimization_barrier(jnp.mean(resid, axis=-1, keepdims=True))
    inv_std = lax.rsqrt(lax.optimization_barrier(jnp.mean(center * center, axis=-1, keepdims=True)) + norm_eps)
    normed = center * inv_std
    return (normed * (1.0 + gain) + shift, normed, inv_std)

def norm_back(upstream, normed, inv_std, gain):
    scaled = upstream * (1.0 + gain)
    return inv_std * (scaled - lax.optimization_barrier(jnp.mean(scaled, axis=-1, keepdims=True)) - normed * lax.optimization_barrier(jnp.mean(scaled * normed, axis=-1, keepdims=True)))

def gelu_pair(before):
    cumul = 0.5 * (1.0 + lax.erf(before * 0.7071067811865476))
    density = jnp.exp(-0.5 * before * before) * 0.3989422804014327
    return (before * cumul, cumul + before * density)

def adamw_step(weight, moments, grad, decay):
    first = beta_one * moments[0] + (1.0 - beta_one) * grad
    second = beta_two * moments[1] + (1.0 - beta_two) * grad * grad
    scale_one = 1.0 - beta_one ** STEP
    scale_two = 1.0 - beta_two ** STEP
    update = first / scale_one / (jnp.sqrt(second / scale_two) + adam_eps) + decay * weight
    return (weight - learn_rate * update, jnp.stack([first, second]))

def group_sum(left_groups, right_groups):

    def add_group(total, pair):
        part = jnp.dot(pair[0], pair[1], preferred_element_type=jnp.float32)
        rounded = lax.optimization_barrier(part.astype(jnp.bfloat16))
        return (total + rounded.astype(jnp.float32), None)
    start = jnp.zeros((left_groups.shape[1], right_groups.shape[2]), jnp.float32)
    total, _ = lax.scan(add_group, start, (left_groups, right_groups))
    return total

def column_groups(matrix, group_width):
    return matrix.reshape(matrix.shape[0], -1, group_width).transpose(1, 0, 2)

def row_groups(matrix, group_width):
    return matrix.reshape(-1, group_width, matrix.shape[1])

def head_view(matrix):
    return matrix.astype(jnp.float32).reshape(SEQS_DEV, L, H, HD)

def member_pass(block_rows, upstream, member_lengths, qkv_w, proj_w, expand_w, reduce_w, query_bias, value_bias, hidden_bias, vectors):
    half = jnp.bfloat16
    count = block_rows.shape[0]
    positions = jnp.arange(count, dtype=jnp.int32)
    live = positions % L < member_lengths[positions // L]
    head_width = D // N_TENSOR
    unit_width = FF // N_TENSOR
    block_f = block_rows.astype(jnp.float32)
    projected = jnp.einsum('td,jde->jte', block_f, qkv_w.astype(jnp.float32))
    query = (projected[0] + query_bias).astype(half)
    keys = projected[1].astype(half)
    values = (projected[2] + value_bias).astype(half)
    query_h = head_view(query)
    keys_h = head_view(keys)
    values_h = head_view(values)
    key_mask = live.reshape(SEQS_DEV, 1, 1, L)
    scores = jnp.einsum('sqhe,skhe->shqk', query_h, keys_h) * HD ** (-0.5)
    scores = jnp.where(key_mask, scores, -jnp.inf)
    row_max = lax.optimization_barrier(jnp.max(scores, axis=-1, keepdims=True))
    exponent = jnp.exp(scores - row_max)
    denominator = lax.optimization_barrier(jnp.sum(exponent, axis=-1, keepdims=True))
    log_total = row_max + jnp.log(denominator)
    weights_b = (exponent / denominator).astype(half)
    heads_out = jnp.einsum('shqk,skhe->sqhe', weights_b.astype(jnp.float32), values_h)
    heads_out = heads_out.astype(half).reshape(count, D)
    attn = group_sum(column_groups(heads_out, head_width), row_groups(proj_w, head_width))
    resid_one = block_f + attn + vectors[0]
    hidden_f, normed_one, inv_one = layer_norm(resid_one, vectors[1], vectors[2])
    hidden_b = hidden_f.astype(half)
    before = jnp.dot(hidden_b, expand_w, preferred_element_type=jnp.float32) + hidden_bias
    active, slope = gelu_pair(before)
    active_b = active.astype(half)
    ffn = group_sum(column_groups(active_b, unit_width), row_groups(reduce_w, unit_width))
    resid_two = hidden_f + ffn + vectors[3]
    out_f, normed_two, inv_two = layer_norm(resid_two, vectors[4], vectors[5])
    grad_out = jnp.where(live[:, None], upstream.astype(jnp.float32), 0.0)
    d_two = norm_back(grad_out, normed_two, inv_two, vectors[4])
    d_two_b = d_two.astype(half)
    g_reduce = jnp.dot(active_b.T, d_two_b, preferred_element_type=jnp.float32)
    d_pre = jnp.dot(d_two_b, reduce_w.T, preferred_element_type=jnp.float32) * slope
    g_hidden_bias = lax.optimization_barrier(jnp.sum(d_pre, axis=0))
    d_pre_b = d_pre.astype(half)
    g_expand = jnp.dot(hidden_b.T, d_pre_b, preferred_element_type=jnp.float32)
    d_hidden = d_two + group_sum(column_groups(d_pre_b, unit_width), row_groups(expand_w.T, unit_width))
    d_one = norm_back(d_hidden, normed_one, inv_one, vectors[1])
    d_one_b = d_one.astype(half)
    g_proj = jnp.dot(heads_out.T, d_one_b, preferred_element_type=jnp.float32)
    d_heads = jnp.dot(d_one_b, proj_w.T, preferred_element_type=jnp.float32).astype(half)
    d_heads_h = head_view(d_heads)
    back_prob = jnp.exp(scores - log_total)
    d_prob = jnp.einsum('sqhe,skhe->shqk', d_heads_h, values_h)
    delta = lax.optimization_barrier(jnp.sum(back_prob * d_prob, axis=-1, keepdims=True))
    d_score = (back_prob * (d_prob - delta) * HD ** (-0.5)).astype(half).astype(jnp.float32)
    back_b = back_prob.astype(half).astype(jnp.float32)
    d_query = jnp.einsum('shqk,skhe->sqhe', d_score, keys_h).reshape(count, D)
    d_keys = jnp.einsum('shqk,sqhe->skhe', d_score, query_h).reshape(count, D)
    d_values = jnp.einsum('shqk,sqhe->skhe', back_b, d_heads_h).reshape(count, D)
    d_stack = jnp.stack([d_query, d_keys, d_values]).astype(half)
    g_qkv = jnp.einsum('td,jte->jde', block_f, d_stack.astype(jnp.float32))
    left = d_stack.reshape(3, count, N_TENSOR, head_width).transpose(2, 1, 0, 3)
    left = left.reshape(N_TENSOR, count, 3 * head_width)
    right = qkv_w.reshape(3, D, N_TENSOR, head_width).transpose(2, 0, 3, 1)
    right = right.reshape(N_TENSOR, 3 * head_width, D)
    d_input = d_one + group_sum(left, right)
    g_vector = jnp.stack([lax.optimization_barrier(jnp.sum(d_one, axis=0)), lax.optimization_barrier(jnp.sum(d_hidden * normed_one, axis=0)), lax.optimization_barrier(jnp.sum(d_hidden, axis=0)), lax.optimization_barrier(jnp.sum(d_two, axis=0)), lax.optimization_barrier(jnp.sum(grad_out * normed_two, axis=0)), lax.optimization_barrier(jnp.sum(grad_out, axis=0))])
    grads = (g_qkv, g_proj, g_expand, g_reduce, lax.optimization_barrier(jnp.sum(d_query, axis=0)), lax.optimization_barrier(jnp.sum(d_values, axis=0)), g_hidden_bias, g_vector)
    return ((out_f.astype(half), d_input.astype(half)), grads)

def reference(block_in, cotangent, lengths, qkv_weight, proj_weight, expand_weight, reduce_weight, split_bias, vector_params, qkv_moments, proj_moments, expand_moments, reduce_moments, bias_moments, vector_moments):
    half = jnp.bfloat16
    qkv_w = qkv_weight.astype(half)
    proj_w = proj_weight.astype(half)
    expand_w = expand_weight.astype(half)
    reduce_w = reduce_weight.astype(half)
    bias_f = lax.optimization_barrier(split_bias.astype(half)).astype(jnp.float32)
    query_bias = bias_f[:, :HD].reshape(D)
    value_bias = bias_f[:, HD:2 * HD].reshape(D)
    hidden_bias = bias_f[:, 2 * HD:].reshape(FF)
    vectors = lax.optimization_barrier(vector_params.astype(half)).astype(jnp.float32)

    def member(carry, item):
        outputs, grads = member_pass(item[0], item[1], item[2], qkv_w, proj_w, expand_w, reduce_w, query_bias, value_bias, hidden_bias, vectors)
        return (jax.tree.map(jnp.add, carry, grads), outputs)
    zeros = (jnp.zeros((3, D, D), jnp.float32), jnp.zeros((D, D), jnp.float32), jnp.zeros((D, FF), jnp.float32), jnp.zeros((FF, D), jnp.float32), jnp.zeros((D,), jnp.float32), jnp.zeros((D,), jnp.float32), jnp.zeros((FF,), jnp.float32), jnp.zeros((6, D), jnp.float32))
    items = (block_in.reshape(N_DP, TOK_DEV, D), cotangent.reshape(N_DP, TOK_DEV, D), lengths.reshape(N_DP, SEQS_DEV))
    sums, outputs = lax.scan(member, zeros, items)
    g_qkv, g_proj, g_expand, g_reduce, g_query, g_value, g_hidden, g_vector = sums
    g_split = jnp.concatenate([g_query.reshape(H, HD), g_value.reshape(H, HD), g_hidden.reshape(H, FF // H)], axis=1)
    qkv_new, qkv_state = adamw_step(qkv_weight, qkv_moments, g_qkv, decay_rate)
    proj_new, proj_state = adamw_step(proj_weight, proj_moments, g_proj, decay_rate)
    expand_new, expand_state = adamw_step(expand_weight, expand_moments, g_expand, decay_rate)
    reduce_new, reduce_state = adamw_step(reduce_weight, reduce_moments, g_reduce, decay_rate)
    bias_new, bias_state = adamw_step(split_bias, bias_moments, g_split, 0.0)
    vector_new, vector_state = adamw_step(vector_params, vector_moments, g_vector, 0.0)
    return (outputs[0].reshape(TOKENS, D), outputs[1].reshape(TOKENS, D), g_qkv, g_proj, g_expand, g_reduce, g_split, g_vector, qkv_new, proj_new, expand_new, reduce_new, bias_new, vector_new, qkv_state, proj_state, expand_state, reduce_state, bias_state, vector_state)
```

```python
import jax
import jax.numpy as jnp
from jax import lax
from jax.experimental import pallas as pl
from jax.experimental.pallas import tpu as pltpu
from jax.sharding import Mesh
from jax.sharding import PartitionSpec as P

L = 512
STEP = 10
HD = 64
LANES = 128


norm_eps = 1e-05
beta_one = 0.9
beta_two = 0.999
learn_rate = 0.02
decay_rate = 0.01
adam_eps = 1e-08
half = jnp.bfloat16
single = jnp.float32


def layer_norm(resid, gain, shift):
    center = resid - jnp.mean(resid, axis=-1, keepdims=True)
    inv_std = lax.rsqrt(jnp.mean(center * center, axis=-1, keepdims=True) + norm_eps)
    normed = center * inv_std
    return (normed * (1.0 + gain) + shift, normed, inv_std)


def norm_back(upstream, normed, inv_std, gain):
    scaled = upstream * (1.0 + gain)
    return inv_std * (
        scaled
        - jnp.mean(scaled, axis=-1, keepdims=True)
        - normed * jnp.mean(scaled * normed, axis=-1, keepdims=True)
    )


def gelu_pair(before):
    cumul = 0.5 * (1.0 + lax.erf(before * 0.7071067811865476))
    density = jnp.exp(-0.5 * before * before) * 0.3989422804014327
    return (before * cumul, cumul + before * density)


def adamw_step(weight, moments, grad, decay):
    first_one = lax.broadcasted_iota(jnp.int32, moments.shape, 0) == 0
    state = jnp.where(
        first_one,
        beta_one * moments + (1.0 - beta_one) * grad,
        beta_two * moments + (1.0 - beta_two) * grad * grad,
    )
    first = beta_one * moments[0] + (1.0 - beta_one) * grad
    second = beta_two * moments[1] + (1.0 - beta_two) * grad * grad
    scale_one = 1.0 - beta_one**STEP
    scale_two = 1.0 - beta_two**STEP
    update = first / scale_one / (jnp.sqrt(second / scale_two) + adam_eps) + decay * weight
    return (weight - learn_rate * update, state)


def dot(a, b, dims, kind=single):
    return lax.dot_general(a, b, (dims, ((), ())), preferred_element_type=single).astype(kind)


NN = ((1,), (0,))
NT = ((1,), (1,))
TN = ((0,), (0,))


def attend_kernel(q_ref, k_ref, v_ref, mask_ref, out_ref, lse_ref):
    lane = lax.broadcasted_iota(jnp.int32, (1, LANES), 1)
    q, k, v = q_ref[...], k_ref[...], v_ref[...]
    out = lse = None
    for head in range(LANES // HD):
        mine = (lane >= head * HD) & (lane < (head + 1) * HD)
        q_h = jnp.where(mine, q, jnp.zeros_like(q))
        scores = dot(q_h, k, NT) * HD ** (-0.5) + mask_ref[...]
        row_max = jnp.max(scores, axis=-1, keepdims=True)
        exponent = jnp.exp(scores - row_max)
        total = jnp.sum(exponent, axis=-1, keepdims=True)
        prob = (exponent / total).astype(half)
        out_h = dot(prob, v, NN)
        lse_h = jnp.broadcast_to(row_max + jnp.log(total), out_h.shape)
        out = out_h if out is None else jnp.where(mine, out_h, out)
        lse = lse_h if lse is None else jnp.where(mine, lse_h, lse)
    out_ref[...] = out.astype(half)
    lse_ref[...] = lse


def attend(projected, mask):
    rows, width = projected.shape
    blocks = width // (3 * LANES)
    block = (rows, LANES)
    return pl.pallas_call(
        attend_kernel,
        grid=(blocks,),
        in_specs=[
            pl.BlockSpec(block, lambda i: (0, i)),
            pl.BlockSpec(block, lambda i: (0, blocks + i)),
            pl.BlockSpec(block, lambda i: (0, 2 * blocks + i)),
            pl.BlockSpec((1, rows), lambda i: (0, 0)),
        ],
        out_specs=[pl.BlockSpec(block, lambda i: (0, i))] * 2,
        out_shape=[
            jax.ShapeDtypeStruct((rows, width // 3), half),
            jax.ShapeDtypeStruct((rows, width // 3), single),
        ],
        cost_estimate=pl.CostEstimate(
            flops=blocks * 8 * rows * rows * LANES,
            bytes_accessed=rows * width * 4,
            transcendentals=blocks * 2 * rows * rows,
        ),
    )(projected, projected, projected, mask)


def attend_back_kernel(q_ref, k_ref, v_ref, up_ref, lse_ref, mask_ref, out_ref, sum_ref):
    block = pl.program_id(0)
    blocks = pl.num_programs(0)
    lane = lax.broadcasted_iota(jnp.int32, (1, LANES), 1)
    q, k, v, up = q_ref[...], k_ref[...], v_ref[...], up_ref[...]
    grads = None
    for head in range(LANES // HD):
        mine = (lane >= head * HD) & (lane < (head + 1) * HD)
        q_h = jnp.where(mine, q, jnp.zeros_like(q))
        up_h = jnp.where(mine, up, jnp.zeros_like(up))
        scores = dot(q_h, k, NT) * HD ** (-0.5) + mask_ref[...]
        prob = jnp.exp(scores - lse_ref[:, head * HD : head * HD + 1])
        d_prob = dot(up_h, v, NT)
        delta = jnp.sum(prob * d_prob, axis=-1, keepdims=True)
        d_score = (prob * (d_prob - delta) * HD ** (-0.5)).astype(half)
        now = (dot(d_score, k, NN), dot(d_score, q, TN), dot(prob.astype(half), up, TN))
        grads = now if grads is None else [jnp.where(mine, a, b) for a, b in zip(now, grads)]
    for j in range(3):
        start = pl.multiple_of((j * blocks + block) * LANES, LANES)
        out_ref[:, pl.ds(start, LANES)] = grads[j].astype(half)
    sum_ref[...] = jnp.concatenate(
        [
            jnp.broadcast_to(jnp.sum(grads[0], axis=0, keepdims=True), (8, LANES)),
            jnp.broadcast_to(jnp.sum(grads[2], axis=0, keepdims=True), (8, LANES)),
        ],
        axis=0,
    )


def attend_back(projected, upstream, lse, mask):
    rows, width = projected.shape
    blocks = width // (3 * LANES)
    block = (rows, LANES)
    return pl.pallas_call(
        attend_back_kernel,
        grid=(blocks,),
        in_specs=[
            pl.BlockSpec(block, lambda i: (0, i)),
            pl.BlockSpec(block, lambda i: (0, blocks + i)),
            pl.BlockSpec(block, lambda i: (0, 2 * blocks + i)),
            pl.BlockSpec(block, lambda i: (0, i)),
            pl.BlockSpec(block, lambda i: (0, i)),
            pl.BlockSpec((1, rows), lambda i: (0, 0)),
        ],
        out_specs=[
            pl.BlockSpec((rows, width), lambda i: (0, 0)),
            pl.BlockSpec((16, LANES), lambda i: (0, i)),
        ],
        out_shape=[
            jax.ShapeDtypeStruct((rows, width), half),
            jax.ShapeDtypeStruct((16, width // 3), single),
        ],
        cost_estimate=pl.CostEstimate(
            flops=blocks * 20 * rows * rows * LANES,
            bytes_accessed=rows * width * 6,
            transcendentals=blocks * 2 * rows * rows,
        ),
    )(projected, projected, projected, upstream, lse, mask)


def flip(value, axis, bit):
    count = lax.axis_size(axis)
    return lax.ppermute(value, axis, [(i, i ^ bit) for i in range(count)])


def shift(value, axis, step):
    count = lax.axis_size(axis)
    return lax.ppermute(value, axis, [(i, (i + step) % count) for i in range(count)])


def bits_of(count):
    return [1 << i for i in range(count.bit_length() - 1)]


def gather_dp(block, order, axis):
    held = [0]
    pieces = {0: block}
    now = block
    for bit in order:
        other = flip(now, "dp", bit)
        size = block.shape[axis]
        for i, j in enumerate(held):
            pieces[j ^ bit] = lax.slice_in_dim(other, i * size, (i + 1) * size, axis=axis)
        now = jnp.concatenate([now, other], axis)
        held = held + [j ^ bit for j in held]
    if held == sorted(held):
        return now
    return jnp.concatenate([pieces[j] for j in range(len(held))], axis)


def scatter_dp(grad, order, axis):
    count = lax.axis_size("dp")
    size = grad.shape[axis] // count
    held = list(range(count))
    now = grad

    def pick(value, wanted):
        if wanted == list(range(wanted[0], wanted[0] + len(wanted))):
            return lax.slice_in_dim(value, wanted[0] * size, (wanted[-1] + 1) * size, axis=axis)
        return jnp.concatenate(
            [lax.slice_in_dim(value, i * size, (i + 1) * size, axis=axis) for i in wanted], axis
        )

    for bit in order:
        keep = [i for i, j in enumerate(held) if not j & bit]
        send = [i for i, j in enumerate(held) if j & bit]
        other = flip(pick(now, send), "dp", bit)
        now = (pick(now, keep).astype(single) + other.astype(single)).astype(now.dtype)
        held = [j for j in held if not j & bit]
    return now


def gather_z(shard):
    return [shard] + [shift(shard, "z", r) for r in range(1, lax.axis_size("z"))]


def scatter_z(slots):
    total = slots[0].astype(single)
    for r in range(1, len(slots)):
        total = total + shift(slots[r], "z", -r).astype(single)
    return total


def sum_members(term):
    now = term.astype(half)
    for bit in bits_of(lax.axis_size("g")):
        total = now.astype(single) + flip(now, "g", bit).astype(single)
        now = total.astype(half)
    return total


def gather_members(rows):
    me = lax.axis_index("g")
    for bit in bits_of(lax.axis_size("g")):
        other = flip(rows, "g", bit)
        rows = jnp.where(
            (me & bit) != 0,
            jnp.concatenate([other, rows], 0),
            jnp.concatenate([rows, other], 0),
        )
    return rows


def scatter_members(term):
    me = lax.axis_index("g")
    now = term.astype(half)
    for bit in reversed(bits_of(lax.axis_size("g"))):
        size = now.shape[0] // 2
        side = ((me & bit) != 0).astype(jnp.int32)
        send = lax.dynamic_slice_in_dim(now, (1 - side) * size, size, 0)
        keep = lax.dynamic_slice_in_dim(now, side * size, size, 0)
        total = keep.astype(single) + flip(send, "g", bit).astype(single)
        now = total.astype(half)
    return total


def reorder(matrix, count, member):
    size = matrix.shape[-1] // count
    return jnp.concatenate(
        [
            lax.dynamic_slice_in_dim(matrix, (member ^ j) * size, size, matrix.ndim - 1)
            for j in range(count)
        ],
        -1,
    )


def on_device(
    block_in,
    cotangent,
    lengths,
    qkv_weight,
    proj_weight,
    expand_weight,
    reduce_weight,
    split_bias,
    vector_params,
    qkv_moments,
    proj_moments,
    expand_moments,
    reduce_moments,
    bias_moments,
    vector_moments,
):
    n_dp, n_z = lax.axis_size("dp"), lax.axis_size("z")
    dp, z, member = lax.axis_index("dp"), lax.axis_index("z"), lax.axis_index("g")
    share = block_in.shape[0]
    model = block_in.shape[1]
    width = qkv_weight.shape[2]
    units = expand_weight.shape[1]
    part = model // n_dp
    heads = split_bias.shape[0]
    bias_part = split_bias.shape[1]
    pair = n_z // 2
    colors = (list(range(pair)), list(range(pair, n_z)))
    bits = bits_of(n_dp)
    orders = (bits, bits[::-1])

    own_q = jnp.concatenate(
        [
            qkv_weight[0].astype(half),
            qkv_weight[1].astype(half),
            qkv_weight[2].astype(half),
            proj_weight.astype(half).T,
        ],
        1,
    )
    own_e = expand_weight.astype(half)
    own_r = reduce_weight.astype(half)
    small = jnp.concatenate(
        [
            vector_params.astype(half),
            jnp.pad(split_bias.astype(half), ((0, 0), (0, part - bias_part))),
        ],
        0,
    )

    def blocks_q(slot):
        return [slot[:, j * width : (j + 1) * width] for j in range(4)]

    slots_q = gather_z(own_q)
    full_q = []
    for color, order in zip(colors, orders):
        split = [blocks_q(slots_q[r]) for r in color]
        joined = jnp.concatenate([split[i][j] for j in range(4) for i in range(len(color))], 1)
        full_q.append(gather_dp(joined, order, 0))
    slots_e = gather_z(own_e)
    full_e = [
        gather_dp(jnp.concatenate([slots_e[r] for r in color], 1), order, 0)
        for color, order in zip(colors, orders)
    ]
    slots_r = gather_z(own_r)
    full_r = [
        gather_dp(jnp.concatenate([slots_r[r] for r in color], 0), order, 1)
        for color, order in zip(colors, orders)
    ]
    small_dp = gather_dp(small[None], bits, 0)
    small_z = gather_z(small_dp)
    vectors = jnp.concatenate([small_dp[j, :6] for j in range(n_dp)], 1).astype(single)

    def bias_of(slot):
        rel = small_z[slot][:, 6:, :bias_part]
        return jnp.concatenate(
            [lax.dynamic_index_in_dim(rel, dp ^ d, 0, keepdims=False) for d in range(n_dp)], 1
        ).astype(single)

    biases = [bias_of(r) for r in range(n_z)]

    length = lax.dynamic_index_in_dim(lengths, z, 0, keepdims=False)
    positions = jnp.arange(L, dtype=jnp.int32)
    live = positions < length
    mask = jnp.where(live, 0.0, -jnp.inf).astype(single)[None, :]

    x_full = gather_members(reorder(block_in, n_dp, dp))
    up_full = gather_members(reorder(cotangent, n_dp, dp))
    cut = 3 * pair * width

    projected, heads_out, lse = [], [], []
    attn_term = 0.0
    for color, weight in zip(colors, full_q):
        q_bias = jnp.concatenate([biases[r][:, :HD].reshape(-1) for r in color])
        v_bias = jnp.concatenate([biases[r][:, HD : 2 * HD].reshape(-1) for r in color])
        bias_row = jnp.concatenate([q_bias, jnp.zeros_like(q_bias), v_bias])
        now = (dot(x_full, weight[:, :cut], NN) + bias_row).astype(half)
        out, log_total = attend(now, mask)
        projected.append(now)
        heads_out.append(out)
        lse.append(log_total)
        attn_term = attn_term + dot(out, weight[:, cut:], NT)
    resid_one = x_full.astype(single) + sum_members(attn_term) + vectors[0]
    hidden_f, normed_one, inv_one = layer_norm(resid_one, vectors[1], vectors[2])
    hidden_b = hidden_f.astype(half)
    active_b, slopes = [], []
    ffn_term = 0.0
    for color, w_e, w_r in zip(colors, full_e, full_r):
        row = jnp.concatenate([biases[r][:, 2 * HD :].reshape(-1) for r in color])
        active, slope = gelu_pair(dot(hidden_b, w_e, NN) + row)
        active_b.append(active.astype(half))
        slopes.append(slope)
        ffn_term = ffn_term + dot(active_b[-1], w_r, NN)
    resid_two = hidden_f + sum_members(ffn_term) + vectors[3]
    out_f, normed_two, inv_two = layer_norm(resid_two, vectors[4], vectors[5])
    grad_out = jnp.where(live[:, None], up_full.astype(single), 0.0)
    d_two = norm_back(grad_out, normed_two, inv_two, vectors[4])
    d_two_b = d_two.astype(half)

    back = tuple(o[::-1] for o in orders)
    reduce_slots, expand_slots, qkv_slots = [], [], []
    d_pre_b, unit_sums = [], []
    hidden_term = 0.0
    for c, order in enumerate(back):
        grad = dot(active_b[c], d_two_b, TN, half)
        got = scatter_dp(grad, order, 1)
        reduce_slots += [got[i * units : (i + 1) * units] for i in range(pair)]
    for c, order in enumerate(back):
        d_pre = dot(d_two_b, full_r[c], NT) * slopes[c]
        unit_sums.append(jnp.sum(d_pre, axis=0))
        d_pre_b.append(d_pre.astype(half))
        grad = dot(hidden_b, d_pre_b[c], TN, half)
        got = scatter_dp(grad, order, 0)
        expand_slots += [got[:, i * units : (i + 1) * units] for i in range(pair)]
        hidden_term = hidden_term + dot(d_pre_b[c], full_e[c], NT)
    d_hidden = d_two + sum_members(hidden_term)
    d_one = norm_back(d_hidden, normed_one, inv_one, vectors[1])
    d_one_b = d_one.astype(half)
    vector_parts = jnp.stack(
        [
            jnp.sum(d_one, axis=0),
            jnp.sum(d_hidden * normed_one, axis=0),
            jnp.sum(d_hidden, axis=0),
            jnp.sum(d_two, axis=0),
            jnp.sum(grad_out * normed_two, axis=0),
            jnp.sum(grad_out, axis=0),
        ]
    )
    input_term = 0.0
    bias_slots = []
    for c, order in enumerate(back):
        weight = full_q[c]
        d_heads = dot(d_one_b, weight[:, cut:], NN, half)
        d_stack, sums = attend_back(projected[c], d_heads, lse[c], mask)
        input_term = input_term + dot(d_stack, weight[:, :cut], NT)
        grad = jnp.concatenate(
            [dot(x_full, d_stack, TN, half), dot(d_one_b, heads_out[c], TN, half)], 1
        )
        got = scatter_dp(grad, order, 0)
        for i in range(pair):
            qkv_slots.append(
                jnp.concatenate(
                    [got[:, (j * pair + i) * width : (j * pair + i + 1) * width] for j in range(4)],
                    1,
                )
            )
            here = slice(i * width, (i + 1) * width)
            bias_slots.append(
                jnp.concatenate(
                    [
                        sums[0, here].reshape(heads, HD),
                        sums[8, here].reshape(heads, HD),
                        unit_sums[c][i * units : (i + 1) * units].reshape(heads, -1),
                    ],
                    1,
                )
            )
    bias_all = jnp.concatenate(bias_slots, 0)
    bias_rel = jnp.stack(
        [
            lax.dynamic_slice_in_dim(bias_all, (dp ^ j) * bias_part, bias_part, 1)
            for j in range(n_dp)
        ]
    )
    bias_rel = jnp.pad(bias_rel, ((0, 0), (0, 0), (0, part - bias_part)))
    vector_rel = vector_parts.reshape(6, n_dp, part).transpose(1, 0, 2)
    small_grad = scatter_dp(jnp.concatenate([vector_rel, bias_rel], 1), bits[::-1], 0)[0]
    packs = [small_grad[:6]] * n_z
    packs = [
        jnp.concatenate([packs[r], small_grad[6 + r * heads : 6 + (r + 1) * heads]], 0)
        for r in range(n_z)
    ]
    landed = jnp.stack([packs[0]] + [shift(packs[r], "z", -r) for r in range(1, n_z)])
    bias_sum = jnp.sum(landed[:, 6:, :bias_part], axis=0)
    vector_sum = lax.dynamic_index_in_dim(landed, (n_z - z) % n_z, 0, keepdims=False)[:6]
    for i in range(1, n_z):
        vector_sum = (
            vector_sum
            + lax.dynamic_index_in_dim(landed, (i + n_z - z) % n_z, 0, keepdims=False)[:6]
        )

    reduce_sum = scatter_z(reduce_slots)
    expand_sum = scatter_z(expand_slots)
    packed = scatter_z(qkv_slots)
    qkv_sum = jnp.stack([packed[:, j * width : (j + 1) * width] for j in range(3)])
    proj_sum = packed[:, 3 * width :].T

    first_row = member * share
    block_out = reorder(lax.dynamic_slice_in_dim(out_f, first_row, share, 0).astype(half), n_dp, dp)
    own_one = lax.dynamic_slice_in_dim(d_one, first_row, share, 0)
    input_grad = reorder((own_one + scatter_members(input_term)).astype(half), n_dp, dp)

    qkv_new, qkv_state = adamw_step(qkv_weight, qkv_moments, qkv_sum, decay_rate)
    proj_new, proj_state = adamw_step(proj_weight, proj_moments, proj_sum, decay_rate)
    expand_new, expand_state = adamw_step(expand_weight, expand_moments, expand_sum, decay_rate)
    reduce_new, reduce_state = adamw_step(reduce_weight, reduce_moments, reduce_sum, decay_rate)
    bias_new, bias_state = adamw_step(split_bias, bias_moments, bias_sum, 0.0)
    vector_new, vector_state = adamw_step(vector_params, vector_moments, vector_sum, 0.0)
    return (
        block_out,
        input_grad,
        qkv_sum,
        proj_sum,
        expand_sum,
        reduce_sum,
        bias_sum,
        vector_sum,
        qkv_new,
        proj_new,
        expand_new,
        reduce_new,
        bias_new,
        vector_new,
        qkv_state,
        proj_state,
        expand_state,
        reduce_state,
        bias_state,
        vector_state,
    )


def solution(mesh):
    n_dp, n_tensor = mesh.devices.shape

    def step(*args):
        share = args[0].shape[0] // (n_dp * n_tensor)
        members = L // share
        inner = Mesh(
            mesh.devices.reshape(n_dp, n_tensor // members, members), ("dp", "z", "g")
        )
        tensor = ("z", "g")
        rows = P(("dp", "z", "g"), None)
        weights = (
            P(None, "dp", tensor),
            P(tensor, "dp"),
            P("dp", tensor),
            P(tensor, "dp"),
            P(tensor, "dp"),
            P(None, "dp"),
        )
        states = (
            P(None, None, "dp", tensor),
            P(None, tensor, "dp"),
            P(None, "dp", tensor),
            P(None, tensor, "dp"),
            P(None, tensor, "dp"),
            P(None, None, "dp"),
        )
        return jax.shard_map(
            on_device,
            mesh=inner,
            in_specs=(rows, rows, P("dp")) + weights + states,
            out_specs=(rows, rows) + weights + weights + states,
            check_vma=False,
        )(*args)

    return step
```

```python
import functools

import jax
import jax.numpy as jnp
from jax import lax
from jax.experimental import pallas as pl
from jax.experimental.pallas import tpu as pltpu
from jax.sharding import Mesh
from jax.sharding import PartitionSpec as P


L = 512
STEP = 10
HD = 64
LANES = 128
GRANT = 20 << 20


norm_eps = 1e-05
beta_one = 0.9
beta_two = 0.999
learn_rate = 0.02
decay_rate = 0.01
adam_eps = 1e-08
half = jnp.bfloat16
single = jnp.float32


def gelu_pair(before):
    cumul = 0.5 * (1.0 + lax.erf(before * 0.7071067811865476))
    density = jnp.exp(-0.5 * before * before) * 0.3989422804014327
    return (before * cumul, cumul + before * density)


def adamw_step(weight, moments, grad, decay):
    first_one = lax.broadcasted_iota(jnp.int32, moments.shape, 0) == 0
    state = jnp.where(
        first_one,
        beta_one * moments + (1.0 - beta_one) * grad,
        beta_two * moments + (1.0 - beta_two) * grad * grad,
    )
    first = beta_one * moments[0] + (1.0 - beta_one) * grad
    second = beta_two * moments[1] + (1.0 - beta_two) * grad * grad
    scale_one = 1.0 - beta_one**STEP
    scale_two = 1.0 - beta_two**STEP
    update = first / scale_one / (jnp.sqrt(second / scale_two) + adam_eps) + decay * weight
    return (weight - learn_rate * update, state)


def dot(a, b, dims, kind=single):
    return lax.dot_general(a, b, (dims, ((), ())), preferred_element_type=single).astype(kind)


def call(kernel, **options):
    params = pltpu.CompilerParams(vmem_limit_bytes=GRANT)
    return pl.pallas_call(kernel, compiler_params=params, **options)


NN = ((1,), (0,))
NT = ((1,), (1,))
TN = ((0,), (0,))


def attend_kernel(q_ref, k_ref, v_ref, mask_ref, out_ref, lse_ref):
    lane = lax.broadcasted_iota(jnp.int32, (1, LANES), 1)
    q, k, v = q_ref[...], k_ref[...], v_ref[...]
    out = lse = None
    for head in range(LANES // HD):
        mine = (lane >= head * HD) & (lane < (head + 1) * HD)
        q_h = jnp.where(mine, q, jnp.zeros_like(q))
        scores = dot(q_h, k, NT) * HD ** (-0.5) + mask_ref[...]
        row_max = jnp.max(scores, axis=-1, keepdims=True)
        exponent = jnp.exp(scores - row_max)
        total = jnp.sum(exponent, axis=-1, keepdims=True)
        prob = (exponent / total).astype(half)
        out_h = dot(prob, v, NN)
        lse_h = jnp.broadcast_to(row_max + jnp.log(total), out_h.shape)
        out = out_h if out is None else jnp.where(mine, out_h, out)
        lse = lse_h if lse is None else jnp.where(mine, lse_h, lse)
    out_ref[...] = out.astype(half)
    lse_ref[...] = lse


def group_block(j, per):
    return lambda i: (0, (i // per) * 4 * per + j * per + i % per)


def attend(projected, mask, per):
    rows, width = projected.shape
    blocks = width // (4 * LANES)
    block = (rows, LANES)
    return call(
        attend_kernel,
        grid=(blocks,),
        in_specs=[pl.BlockSpec(block, group_block(j, per)) for j in range(3)]
        + [pl.BlockSpec((1, rows), lambda i: (0, 0))],
        out_specs=[pl.BlockSpec(block, lambda i: (0, i))] * 2,
        out_shape=[
            jax.ShapeDtypeStruct((rows, width // 4), half),
            jax.ShapeDtypeStruct((rows, width // 4), single),
        ],
        cost_estimate=pl.CostEstimate(
            flops=blocks * 8 * rows * rows * LANES,
            bytes_accessed=rows * width * 4,
            transcendentals=blocks * 2 * rows * rows,
        ),
    )(projected, projected, projected, mask)


def attend_back_kernel(per, q_ref, k_ref, v_ref, up_ref, lse_ref, mask_ref, out_ref, sum_ref):
    block = pl.program_id(0)
    lane = lax.broadcasted_iota(jnp.int32, (1, LANES), 1)
    q, k, v, up = q_ref[...], k_ref[...], v_ref[...], up_ref[...]
    grads = None
    for head in range(LANES // HD):
        mine = (lane >= head * HD) & (lane < (head + 1) * HD)
        q_h = jnp.where(mine, q, jnp.zeros_like(q))
        up_h = jnp.where(mine, up, jnp.zeros_like(up))
        scores = dot(q_h, k, NT) * HD ** (-0.5) + mask_ref[...]
        prob = jnp.exp(scores - lse_ref[:, head * HD : head * HD + 1])
        d_prob = dot(up_h, v, NT)
        delta = jnp.sum(prob * d_prob, axis=-1, keepdims=True)
        d_score = (prob * (d_prob - delta) * HD ** (-0.5)).astype(half)
        now = (dot(d_score, k, NN), dot(d_score, q, TN), dot(prob.astype(half), up, TN))
        grads = now if grads is None else [jnp.where(mine, a, b) for a, b in zip(now, grads)]
    parts = [g.astype(half) for g in grads] + [jnp.zeros_like(q)]
    for j in range(4):
        start = ((block // per) * 4 * per + j * per + block % per) * LANES
        out_ref[:, pl.ds(pl.multiple_of(start, LANES), LANES)] = parts[j]
    row = lax.broadcasted_iota(jnp.int32, (8, LANES), 0)
    for j, grad in enumerate((grads[0], None, grads[2], None)):
        start = ((block // per) * 4 * per + j * per + block % per) * LANES
        total = 0.0 if grad is None else jnp.sum(grad, axis=0, keepdims=True)
        sums = jnp.where(row == 6, total, 0.0)
        sum_ref[:, pl.ds(pl.multiple_of(start, LANES), LANES)] = sums


def attend_back(projected, upstream, lse, mask, per):
    rows, width = projected.shape
    blocks = width // (4 * LANES)
    block = (rows, LANES)
    return call(
        functools.partial(attend_back_kernel, per),
        grid=(blocks,),
        in_specs=[pl.BlockSpec(block, group_block(j, per)) for j in range(3)]
        + [
            pl.BlockSpec(block, lambda i: (0, i)),
            pl.BlockSpec(block, lambda i: (0, i)),
            pl.BlockSpec((1, rows), lambda i: (0, 0)),
        ],
        out_specs=[
            pl.BlockSpec((rows, width), lambda i: (0, 0)),
            pl.BlockSpec((8, width), lambda i: (0, 0)),
        ],
        out_shape=[
            jax.ShapeDtypeStruct((rows, width), half),
            jax.ShapeDtypeStruct((8, width), single),
        ],
        cost_estimate=pl.CostEstimate(
            flops=blocks * 20 * rows * rows * LANES,
            bytes_accessed=rows * width * 6,
            transcendentals=blocks * 2 * rows * rows,
        ),
    )(projected, projected, projected, upstream, lse, mask)


def normal_rows(resid):
    center = resid - jnp.mean(resid, axis=-1, keepdims=True)
    inv_std = lax.rsqrt(jnp.mean(center * center, axis=-1, keepdims=True) + norm_eps)
    return center * inv_std, inv_std


def norm_back(scaled, normed, inv_std):
    return inv_std * (
        scaled
        - jnp.mean(scaled, axis=-1, keepdims=True)
        - normed * jnp.mean(scaled * normed, axis=-1, keepdims=True)
    )


def first_norm_kernel(x_ref, mine_ref, other_ref, vec_ref, hidden_ref, half_ref, normed_ref, inv_ref):
    attn = mine_ref[...].astype(single) + other_ref[...].astype(single)
    resid = x_ref[...].astype(single) + attn + vec_ref[0:1, :]
    normed, inv_std = normal_rows(resid)
    hidden = normed * (1.0 + vec_ref[1:2, :]) + vec_ref[2:3, :]
    hidden_ref[...] = hidden
    half_ref[...] = hidden.astype(half)
    normed_ref[...] = normed
    inv_ref[...] = jnp.broadcast_to(inv_std, inv_ref.shape)


def add_sums(sum_ref, start, terms):
    row = lax.broadcasted_iota(jnp.int32, sum_ref.shape, 0)
    now = jnp.zeros(sum_ref.shape, single)
    for i, term in enumerate(terms):
        total = jnp.sum(term, axis=0, keepdims=True)
        now = now + jnp.where(row == start + i, total, 0.0)

    @pl.when(pl.program_id(0) == 0)
    def _():
        sum_ref[...] = now

    @pl.when(pl.program_id(0) != 0)
    def _():
        sum_ref[...] += now


def second_norm_kernel(
    hidden_ref, mine_ref, other_ref, up_ref, live_ref, vec_ref, out_ref, two_ref, half_ref, sum_ref
):
    ffn = mine_ref[...].astype(single) + other_ref[...].astype(single)
    resid = hidden_ref[...] + ffn + vec_ref[3:4, :]
    normed, inv_std = normal_rows(resid)
    gain = 1.0 + vec_ref[4:5, :]
    out_ref[...] = (normed * gain + vec_ref[5:6, :]).astype(half)
    grad_out = jnp.where(live_ref[:, 0:1] > 0.0, up_ref[...].astype(single), 0.0)
    d_two = norm_back(grad_out * gain, normed, inv_std)
    two_ref[...] = d_two
    half_ref[...] = d_two.astype(half)
    add_sums(sum_ref, 3, [d_two, grad_out * normed, grad_out])


def first_back_kernel(
    two_ref, mine_ref, other_ref, normed_ref, inv_ref, vec_ref, one_ref, half_ref, sum_ref
):
    term = mine_ref[...].astype(single) + other_ref[...].astype(single)
    d_hidden = two_ref[...] + term
    normed = normed_ref[...]
    d_one = norm_back(d_hidden * (1.0 + vec_ref[1:2, :]), normed, inv_ref[:, 0:1])
    one_ref[...] = d_one
    half_ref[...] = d_one.astype(half)
    add_sums(sum_ref, 0, [d_one, d_hidden * normed, d_hidden])


def by_rows(kernel, inputs, outputs, sums):
    rows = inputs[0].shape[0]
    tile = min(rows, 128)

    def spec(shape):
        if shape[0] == rows:
            return pl.BlockSpec((tile, shape[1]), lambda i: (i, 0))
        return pl.BlockSpec(shape, lambda i: (0, 0))

    shapes = [jax.ShapeDtypeStruct((rows, w), kind) for w, kind in outputs]
    shapes += [jax.ShapeDtypeStruct((8, sums), single)] if sums else []
    return call(
        kernel,
        grid=(rows // tile,),
        in_specs=[spec(a.shape) for a in inputs],
        out_specs=[spec(a.shape) for a in shapes],
        out_shape=shapes,
        cost_estimate=pl.CostEstimate(
            flops=40 * rows * inputs[0].shape[1],
            bytes_accessed=20 * rows * inputs[0].shape[1],
            transcendentals=rows,
        ),
    )(*inputs)


def first_grad_kernel(
    size, per, x_ref, stack_ref, one_ref, heads_ref, vec_ref, qv_ref, unit_ref, out_ref
):
    out_ref[0:size, :] = dot(x_ref[...], stack_ref[...], TN, half)
    proj = dot(one_ref[...], heads_ref[...], TN, half)
    span = per * LANES
    for g in range(proj.shape[1] // span):
        start = (4 * g + 3) * span
        out_ref[0:size, start : start + span] = proj[:, g * span : (g + 1) * span]
    small = vec_ref[...] + qv_ref[...] + unit_ref[...]
    blank = jnp.zeros((out_ref.shape[0] - size - 8, small.shape[1]), single)
    out_ref[size:, :] = jnp.concatenate([small, blank], 0).astype(half)


def first_grad(x, stack, one, heads, vec, qv, unit, wanted, size, per, extra):
    rows, width = stack.shape
    first, stride = wanted[0], (wanted[1] - wanted[0] if len(wanted) > 1 else 1)
    assert wanted == [first + i * stride for i in range(len(wanted))]
    return call(
        functools.partial(first_grad_kernel, size, per),
        grid=(len(wanted),),
        in_specs=[
            pl.BlockSpec((rows, size), lambda i: (0, first + i * stride)),
            pl.BlockSpec(stack.shape, lambda i: (0, 0)),
            pl.BlockSpec((rows, size), lambda i: (0, first + i * stride)),
            pl.BlockSpec(heads.shape, lambda i: (0, 0)),
            pl.BlockSpec((8, width), lambda i: (0, first + i * stride)),
            whole_spec(qv.shape),
            whole_spec(unit.shape),
        ],
        out_specs=pl.BlockSpec((size + extra, width), lambda i: (i, 0)),
        out_shape=jax.ShapeDtypeStruct((len(wanted) * (size + extra), width), half),
        cost_estimate=pl.CostEstimate(
            flops=len(wanted) * 2 * rows * size * (width + heads.shape[1]),
            bytes_accessed=rows * width * 4,
            transcendentals=0,
        ),
    )(x, stack, one, heads, vec, qv, unit)


def flip(value, axis, bit):
    count = lax.axis_size(axis)
    return lax.ppermute(value, axis, [(i, i ^ bit) for i in range(count)])


def bits_of(count):
    return [1 << i for i in range(count.bit_length() - 1)]


def cut(value, start, size, axis):
    return lax.slice_in_dim(value, start, start + size, axis=axis)


class Pieces:
    def __init__(self, now, other, order, size, pitch, axis):
        held = [0]
        for bit in order[:-1]:
            held = held + [j ^ bit for j in held]
        self.arrays = (now, other)
        self.where = {}
        for i, j in enumerate(held):
            self.where[j] = (0, i * pitch)
            self.where[j ^ order[-1]] = (1, i * pitch)
        self.size, self.axis = size, axis

    def read(self, refs, j, columns=None):
        side, start = self.where[j]
        if self.axis == 1:
            return refs[side][:, start : start + self.size]
        if columns is None:
            return refs[side][start : start + self.size, :]
        return refs[side][start : start + self.size, columns]


def gather_dp(block, order, axis):
    now = block
    for step, bit in enumerate(order):
        other = flip(now, "dp", bit)
        if step + 1 < len(order):
            now = jnp.concatenate([now, other], axis)
    return now, other


def whole_spec(shape):
    return pl.BlockSpec(shape, lambda i: (0, 0))


def cost(flops, moved):
    return pl.CostEstimate(flops=flops, bytes_accessed=moved, transcendentals=0)


def project_kernel(weight, gelu, x_ref, now_ref, other_ref, row_ref, out_ref, *slope_ref):
    refs = (now_ref, other_ref)
    total = row_ref[...]
    for j in sorted(weight.where):
        x = x_ref[:, j * weight.size : (j + 1) * weight.size]
        total = total + dot(x, weight.read(refs, j), NN)
    if gelu:
        active, slope = gelu_pair(total)
        out_ref[...] = active.astype(half)
        slope_ref[0][...] = slope
    else:
        out_ref[...] = total.astype(half)


def project(x, weight, row, gelu):
    rows, width = x.shape[0], row.shape[0]
    tile = min(width, 256)
    column = lambda i: (0, i)
    shapes = [jax.ShapeDtypeStruct((rows, width), half)]
    if gelu:
        shapes.append(jax.ShapeDtypeStruct((rows, width), single))
    out = call(
        functools.partial(project_kernel, weight, gelu),
        grid=(width // tile,),
        in_specs=[whole_spec(x.shape)]
        + [pl.BlockSpec((a.shape[0], tile), column) for a in weight.arrays]
        + [pl.BlockSpec((1, tile), column)],
        out_specs=[pl.BlockSpec((rows, tile), column) for _ in shapes],
        out_shape=shapes,
        cost_estimate=cost(2 * rows * x.shape[1] * width, 4 * rows * width),
    )(x, *weight.arrays, row[None, :])
    return out if gelu else out[0]


def back_units_kernel(weight, up_ref, now_ref, other_ref, slope_ref, out_ref, sum_ref):
    refs = (now_ref, other_ref)
    total = 0.0
    for j in sorted(weight.where):
        up = up_ref[:, j * weight.size : (j + 1) * weight.size]
        total = total + dot(up, weight.read(refs, j), NT)
    d_pre = total * slope_ref[...]
    out_ref[...] = d_pre.astype(half)
    row = lax.broadcasted_iota(jnp.int32, sum_ref.shape, 0)
    sum_ref[...] = jnp.where(row == 7, jnp.sum(d_pre, axis=0, keepdims=True), 0.0)


def back_units(upstream, weight, slope):
    rows, width = slope.shape
    tile = min(width, 256)
    column = lambda i: (0, i)
    return call(
        functools.partial(back_units_kernel, weight),
        grid=(width // tile,),
        in_specs=[whole_spec(upstream.shape)]
        + [pl.BlockSpec((tile, a.shape[1]), lambda i: (i, 0)) for a in weight.arrays]
        + [pl.BlockSpec((rows, tile), column)],
        out_specs=[pl.BlockSpec((rows, tile), column), pl.BlockSpec((8, tile), column)],
        out_shape=[
            jax.ShapeDtypeStruct((rows, width), half),
            jax.ShapeDtypeStruct((8, width), single),
        ],
        cost_estimate=cost(2 * rows * upstream.shape[1] * width, 6 * rows * width),
    )(upstream, *weight.arrays, slope)


def blend_kernel(weights, columns, dims, *refs):
    out_ref = refs[-1]
    size = weights[0].size
    for j in sorted(weights[0].where):
        total = 0.0
        for c, weight in enumerate(weights):
            left, pair = refs[3 * c], refs[3 * c + 1 : 3 * c + 3]
            if columns is None:
                total = total + dot(left[...], weight.read(pair, j), dims)
                continue
            span = columns[0].stop - columns[0].start
            for g, window in enumerate(columns):
                part = left[:, g * span : (g + 1) * span]
                total = total + dot(part, weight.read(pair, j, window), dims)
        out_ref[:, j * size : (j + 1) * size] = total.astype(half)


def blend(lefts, weights, dims, columns=None):
    rows = lefts[0].shape[0]
    width = weights[0].size * len(weights[0].where)
    tile = min(rows, 256)
    inputs, specs = [], []
    for left, weight in zip(lefts, weights):
        inputs += [left, *weight.arrays]
        specs.append(pl.BlockSpec((tile, left.shape[1]), lambda i: (i, 0)))
        specs += [whole_spec(a.shape) for a in weight.arrays]
    return call(
        functools.partial(blend_kernel, weights, columns, dims),
        grid=(rows // tile,),
        in_specs=specs,
        out_specs=pl.BlockSpec((tile, width), lambda i: (i, 0)),
        out_shape=jax.ShapeDtypeStruct((rows, width), half),
        cost_estimate=cost(4 * rows * width * lefts[0].shape[1], 8 * rows * width),
    )(*inputs)


def back_heads_kernel(weight, columns, up_ref, now_ref, other_ref, out_ref):
    refs = (now_ref, other_ref)
    span = columns[0].stop - columns[0].start
    for g, window in enumerate(columns):
        total = 0.0
        for j in sorted(weight.where):
            up = up_ref[:, j * weight.size : (j + 1) * weight.size]
            total = total + dot(up, weight.read(refs, j, window), NN)
        out_ref[:, g * span : (g + 1) * span] = total.astype(half)


def back_heads(upstream, weight, columns):
    rows = upstream.shape[0]
    width = sum(w.stop - w.start for w in columns)
    return call(
        functools.partial(back_heads_kernel, weight, columns),
        grid=(1,),
        in_specs=[whole_spec(a.shape) for a in (upstream, *weight.arrays)],
        out_specs=whole_spec((rows, width)),
        out_shape=jax.ShapeDtypeStruct((rows, width), half),
        cost_estimate=cost(2 * rows * upstream.shape[1] * width, 8 * rows * width),
    )(upstream, *weight.arrays)


def block_grad_kernel(left_ref, right_ref, out_ref):
    out_ref[...] = dot(left_ref[...], right_ref[...], TN, half)


def block_grad(left, right, wanted, size, rows_cut):
    count = len(wanted)
    first, stride = wanted[0], (wanted[1] - wanted[0] if count > 1 else 1)
    assert wanted == [first + i * stride for i in range(count)]
    rows = left.shape[0]
    chosen = pl.BlockSpec((rows, size), lambda i: (0, first + i * stride))
    if rows_cut:
        specs = [chosen, whole_spec(right.shape)]
        block, index = (size, right.shape[1]), lambda i: (i, 0)
        shape = (count * size, right.shape[1])
    else:
        specs = [whole_spec(left.shape), chosen]
        block, index = (left.shape[1], size), lambda i: (0, i)
        shape = (left.shape[1], count * size)
    return call(
        block_grad_kernel,
        grid=(count,),
        in_specs=specs,
        out_specs=pl.BlockSpec(block, index),
        out_shape=jax.ShapeDtypeStruct(shape, half),
        cost_estimate=cost(2 * rows * shape[0] * shape[1], 4 * shape[0] * shape[1]),
    )(left, right)


def halves(members, bit):
    return [j for j in members if j & bit], [j for j in members if not j & bit]


def scatter_dp(away, stay, order, axis):
    held = list(range(lax.axis_size("dp")))
    for step, bit in enumerate(order):
        other = flip(away, "dp", bit)
        held = halves(held, bit)[1]
        if step + 1 == len(order):
            return (stay.astype(single) + other.astype(single)).astype(half)
        size = stay.shape[axis] // len(held)

        def pick(value, wanted):
            parts = [cut(value, held.index(j) * size, size, axis) for j in wanted]
            return parts[0] if len(parts) == 1 else jnp.concatenate(parts, axis)

        def added(wanted):
            total = pick(stay, wanted).astype(single) + pick(other, wanted).astype(single)
            return total.astype(half)

        away, stay = (added(part) for part in halves(held, order[step + 1]))


def gather_z(shard, axis):
    bits = bits_of(lax.axis_size("z"))
    now = shard
    for bit in bits[:-1]:
        now = jnp.concatenate([now, flip(now, "z", bit)], axis)
    return now, flip(now, "z", bits[-1])


def scatter_z(colors, axis):
    bits = bits_of(lax.axis_size("z"))
    held = list(range(1 << len(bits)))
    size = colors[0].shape[axis] * 2 // len(held)
    slots = [cut(color, i * size, size, axis) for color in colors for i in range(len(held) // 2)]
    for bit in bits:
        leave, stay = halves(held, bit)
        parts = [[slots[held.index(r)] for r in group] for group in (leave, stay)]
        away, keep = (p[0] if len(p) == 1 else jnp.concatenate(p, axis) for p in parts)
        other = flip(away, "z", bit)
        if bit == bits[-1]:
            return keep, other
        total = (keep.astype(single) + other.astype(single)).astype(half)
        held = stay
        slots = [cut(total, i * size, size, axis) for i in range(len(held))]


def added(pair):
    return pair[0].astype(single) + pair[1].astype(single)


def first_update_kernel(
    keep_ref, other_ref, qkv_ref, qkv_m_ref, proj_ref, proj_m_ref,
    sum_ref, proj_sum_ref, new_ref, proj_new_ref, state_ref, proj_state_ref, small_ref,
):
    size, width = qkv_ref.shape[1:]
    grad = keep_ref[...].astype(single) + other_ref[...].astype(single)
    small_ref[...] = grad[size:]

    def step(weight, first, second, total):
        first = beta_one * first + (1.0 - beta_one) * total
        second = beta_two * second + (1.0 - beta_two) * total * total
        scale_one = 1.0 - beta_one**STEP
        scale_two = 1.0 - beta_two**STEP
        update = first / scale_one / (jnp.sqrt(second / scale_two) + adam_eps)
        return weight - learn_rate * (update + decay_rate * weight), first, second

    for j in range(3):
        total = grad[:size, j * width : (j + 1) * width]
        sum_ref[j] = total
        new, first, second = step(qkv_ref[j], qkv_m_ref[0, j], qkv_m_ref[1, j], total)
        new_ref[j] = new
        state_ref[0, j] = first
        state_ref[1, j] = second
    total = grad[:size, 3 * width :].T
    proj_sum_ref[...] = total
    new, first, second = step(proj_ref[...], proj_m_ref[0], proj_m_ref[1], total)
    proj_new_ref[...] = new
    proj_state_ref[0] = first
    proj_state_ref[1] = second


def first_update(pair, qkv, qkv_m, proj, proj_m):
    extra = pair[0].shape[0] - qkv.shape[1]
    shapes = [a.shape for a in (qkv, proj, qkv, proj, qkv_m, proj_m)]
    shapes.append((extra, pair[0].shape[1]))
    operands = (*pair, qkv, qkv_m, proj, proj_m)

    def full(shape):
        return pl.BlockSpec(shape, lambda i: (0,) * len(shape))

    return call(
        first_update_kernel,
        grid=(1,),
        in_specs=[full(a.shape) for a in operands],
        out_specs=[full(shape) for shape in shapes],
        out_shape=[jax.ShapeDtypeStruct(shape, single) for shape in shapes],
        cost_estimate=cost(20 * qkv.size, 40 * qkv.size),
    )(*operands)


def sum_members(term):
    now = term
    bits = bits_of(lax.axis_size("g"))
    for bit in bits:
        other = flip(now, "g", bit)
        if bit != bits[-1]:
            now = (now.astype(single) + other.astype(single)).astype(half)
    return now, other


def gather_members(rows):
    me = lax.axis_index("g")
    for bit in bits_of(lax.axis_size("g")):
        other = flip(rows, "g", bit)
        rows = jnp.where(
            (me & bit) != 0,
            jnp.concatenate([other, rows], 0),
            jnp.concatenate([rows, other], 0),
        )
    return rows


def scatter_members(term):
    me = lax.axis_index("g")
    now = term.astype(half)
    for bit in reversed(bits_of(lax.axis_size("g"))):
        size = now.shape[0] // 2
        side = ((me & bit) != 0).astype(jnp.int32)
        send = lax.dynamic_slice_in_dim(now, (1 - side) * size, size, 0)
        keep = lax.dynamic_slice_in_dim(now, side * size, size, 0)
        total = keep.astype(single) + flip(send, "g", bit).astype(single)
        now = total.astype(half)
    return total


def reorder(matrix, count, member):
    size = matrix.shape[-1] // count
    return jnp.concatenate(
        [
            lax.dynamic_slice_in_dim(matrix, (member ^ j) * size, size, matrix.ndim - 1)
            for j in range(count)
        ],
        -1,
    )


def layer_step(
    block_in,
    cotangent,
    lengths,
    qkv_weight,
    proj_weight,
    expand_weight,
    reduce_weight,
    split_bias,
    vector_params,
    qkv_moments,
    proj_moments,
    expand_moments,
    reduce_moments,
    bias_moments,
    vector_moments,
):
    n_dp, n_z = lax.axis_size("dp"), lax.axis_size("z")
    dp, z, member = lax.axis_index("dp"), lax.axis_index("z"), lax.axis_index("g")
    share = block_in.shape[0]
    model = block_in.shape[1]
    width = qkv_weight.shape[2]
    part = model // n_dp
    heads = split_bias.shape[0]
    bias_part = split_bias.shape[1]
    pair = n_z // 2
    ganged = 1 if width % LANES == 0 else pair
    gang = ganged * width
    per = gang // LANES
    up = bits_of(n_dp)
    down = up[::-1]
    order_q, order_e, order_r = (up, up), (down, up), (down, up)
    extra = -(-max(6 + heads, 8) // 16) * 16

    def wide(rows, count):
        return jnp.pad(rows, ((0, 0), (0, count - rows.shape[1])))

    small = jnp.concatenate(
        [
            wide(vector_params.astype(half), 4 * width),
            wide(split_bias.astype(half), 4 * width),
            jnp.zeros((extra - 6 - heads, 4 * width), half),
        ],
        0,
    )
    own_q = jnp.concatenate(
        [qkv_weight[j].astype(half) for j in range(3)] + [proj_weight.astype(half).T], 1
    )
    own_q = jnp.concatenate([own_q, small], 0)
    own_e = expand_weight.astype(half)
    own_r = reduce_weight.astype(half)

    weight_q, weight_e, weight_r, small_q = [], [], [], []

    def ganged_columns(matrix):
        if ganged == 1:
            return matrix
        cut_up = matrix.reshape(matrix.shape[0], -1, ganged, 4, width)
        return cut_up.transpose(0, 1, 3, 2, 4).reshape(matrix.shape)

    for c, block in enumerate(gather_z(own_q, 1)):
        arrays = gather_dp(block, order_q[c], 0)
        held = Pieces(*arrays, order_q[c], extra, part + extra, 0)
        small_q.append(
            [
                cut(arrays[held.where[j][0]], held.where[j][1] + part, extra, 0)
                for j in range(n_dp)
            ]
        )
        arrays = [ganged_columns(a) for a in arrays]
        weight_q.append(Pieces(*arrays, order_q[c], part, part + extra, 0))
    for c, block in enumerate(gather_z(own_e, 1)):
        arrays = gather_dp(block, order_e[c], 0)
        weight_e.append(Pieces(*arrays, order_e[c], part, part, 0))
    for c, block in enumerate(gather_z(own_r, 0)):
        arrays = gather_dp(block, order_r[c], 1)
        weight_r.append(Pieces(*arrays, order_r[c], part, part, 1))

    vectors = jnp.concatenate([small_q[0][j][:6, :part] for j in range(n_dp)], 1)
    vectors = jnp.pad(vectors.astype(single), ((0, 2), (0, 0)))
    mine_at = jnp.arange(n_dp, dtype=jnp.int32)
    picked = ((mine_at[:, None] ^ dp) == mine_at[None, :]).astype(half)

    def biases_of(small_rows):
        rel = jnp.stack([p[6 : 6 + heads] for p in small_rows])
        rel = rel.reshape(n_dp, heads, pair, 4 * width)[..., :bias_part]
        rows = dot(picked, rel.reshape(n_dp, -1), NN).reshape(n_dp, heads, pair, bias_part)
        return rows.transpose(2, 1, 0, 3).reshape(pair, heads, -1)

    length = lax.dynamic_index_in_dim(lengths, z, 0, keepdims=False)
    live = jnp.arange(L, dtype=jnp.int32) < length
    mask = jnp.where(live, 0.0, -jnp.inf).astype(single)[None, :]
    live_rows = jnp.broadcast_to(live[:, None].astype(single), (L, LANES))

    x_full = gather_members(reorder(block_in, n_dp, dp))
    up_full = gather_members(reorder(cotangent, n_dp, dp))

    projected, heads_out, lse, bias_rows = [], [], [], []
    groups = pair // ganged
    out_columns = [slice((4 * i + 3) * gang, (4 * i + 4) * gang) for i in range(groups)]
    for c in range(2):
        if c:
            small_q[c], projected[0] = lax.optimization_barrier((small_q[c], projected[0]))
        bias_rows.append(biases_of(small_q[c]))
        rows = bias_rows[c].reshape(groups, ganged, heads, -1)
        q_bias = rows[..., :HD].reshape(groups, gang)
        v_bias = rows[..., HD : 2 * HD].reshape(groups, gang)
        nothing = jnp.zeros_like(q_bias)
        row = jnp.concatenate([q_bias, nothing, v_bias, nothing], 1).reshape(-1)
        projected.append(project(x_full, weight_q[c], row, False))
        out, log_total = attend(projected[c], mask, per)
        heads_out.append(out)
        lse.append(log_total)
    attn_term = blend(heads_out, weight_q, NT, out_columns)
    mine, other = sum_members(attn_term)
    hidden_f, hidden_b, normed_one, inv_one = by_rows(
        first_norm_kernel,
        (x_full, mine, other, vectors),
        ((model, single), (model, half), (model, single), (LANES, single)),
        0,
    )
    active_b, slopes = [], []
    for c in range(2):
        row = bias_rows[c][..., 2 * HD :].reshape(-1)
        active, slope = project(hidden_b, weight_e[c], row, True)
        active_b.append(active)
        slopes.append(slope)
    ffn_term = blend(active_b, weight_r, NN)
    mine, other = sum_members(ffn_term)
    out_b, d_two, d_two_b, sums_two = by_rows(
        second_norm_kernel,
        (hidden_f, mine, other, up_full, live_rows, vectors),
        ((model, half), (model, single), (model, half)),
        model,
    )

    members = list(range(n_dp))
    firsts = (down[0], up[0])
    back = (down, up)
    got_r, got_e, got_q = [], [], []
    sent_r = []
    for c in range(2):
        sent_r.append(block_grad(active_b[c], d_two_b, halves(members, firsts[c])[0], part, False))
    for c in range(2):
        kept = block_grad(active_b[c], d_two_b, halves(members, firsts[c])[1], part, False)
        got_r.append(scatter_dp(sent_r[c], kept, back[c], 1))
    unit_sums, d_pre_b = [], []
    for c in range(2):
        d_pre, sums = back_units(d_two_b, weight_r[c], slopes[c])
        unit_sums.append(sums)
        d_pre_b.append(d_pre)
    hidden_term = blend(d_pre_b, weight_e, NT)
    for c in range(2):
        leave, kept = halves(members, firsts[c])
        leave = block_grad(hidden_b, d_pre_b[c], leave, part, True)
        kept = block_grad(hidden_b, d_pre_b[c], kept, part, True)
        got_e.append(scatter_dp(leave, kept, back[c], 0))
    mine, other = sum_members(hidden_term)
    d_one, d_one_b, sums_one = by_rows(
        first_back_kernel,
        (d_two, mine, other, normed_one, inv_one, vectors),
        ((model, single), (model, half)),
        model,
    )
    vec = (sums_one + sums_two).reshape(8, n_dp, 1, part)
    vec = jnp.pad(vec, ((0, 0), (0, 0), (0, 0), (0, 4 * width - part)))
    vec = jnp.broadcast_to(vec, (8, n_dp, pair, 4 * width)).reshape(8, -1)
    vec = ganged_columns(vec)
    stacks = []
    for c in range(2):
        d_heads = back_heads(d_one_b, weight_q[c], out_columns)
        d_stack, sums = attend_back(projected[c], d_heads, lse[c], mask, per)
        stacks.append(d_stack)
        unit = ganged_columns(unit_sums[c])
        leave, kept = halves(members, firsts[c])
        operands = (x_full, d_stack, d_one_b, heads_out[c], vec, sums, unit)
        leave = first_grad(*operands, leave, part, per, extra)
        kept = first_grad(*operands, kept, part, per, extra)
        got_q.append(scatter_dp(leave, kept, back[c], 0))
    if ganged > 1:
        got_q = [
            g.reshape(part + extra, -1, 4, ganged, width)
            .transpose(0, 1, 3, 2, 4)
            .reshape(part + extra, -1)
            for g in got_q
        ]

    reduce_sum = added(scatter_z(got_r, 0))
    expand_sum = added(scatter_z(got_e, 1))
    qkv_sum, proj_sum, qkv_new, proj_new, qkv_state, proj_state, packed = first_update(
        scatter_z(got_q, 1), qkv_weight, qkv_moments, proj_weight, proj_moments
    )
    vector_sum = packed[:6, :part]
    bias_all = jnp.concatenate(
        [
            packed[6, :width].reshape(heads, HD),
            packed[6, 2 * width : 3 * width].reshape(heads, HD),
            packed[7].reshape(heads, -1),
        ],
        1,
    )
    bias_sum = lax.dynamic_slice_in_dim(bias_all, dp * bias_part, bias_part, 1)

    out_b, stacks = lax.optimization_barrier((out_b, stacks))
    input_term = blend(stacks, weight_q, NT)
    first_row = member * share
    block_out = reorder(lax.dynamic_slice_in_dim(out_b, first_row, share, 0), n_dp, dp)
    own_one = lax.dynamic_slice_in_dim(d_one, first_row, share, 0)
    input_grad = reorder((own_one + scatter_members(input_term)).astype(half), n_dp, dp)

    expand_new, expand_state = adamw_step(expand_weight, expand_moments, expand_sum, decay_rate)
    reduce_new, reduce_state = adamw_step(reduce_weight, reduce_moments, reduce_sum, decay_rate)
    bias_new, bias_state = adamw_step(split_bias, bias_moments, bias_sum, 0.0)
    vector_new, vector_state = adamw_step(vector_params, vector_moments, vector_sum, 0.0)
    return (
        block_out,
        input_grad,
        qkv_sum,
        proj_sum,
        expand_sum,
        reduce_sum,
        bias_sum,
        vector_sum,
        qkv_new,
        proj_new,
        expand_new,
        reduce_new,
        bias_new,
        vector_new,
        qkv_state,
        proj_state,
        expand_state,
        reduce_state,
        bias_state,
        vector_state,
    )


def solution(mesh):
    n_dp, n_tensor = mesh.devices.shape

    def step(*args):
        share = args[0].shape[0] // (n_dp * n_tensor)
        members = L // share
        inner = Mesh(
            mesh.devices.reshape(n_dp, n_tensor // members, members), ("dp", "z", "g")
        )
        tensor = ("z", "g")
        rows = P(("dp", "z", "g"), None)
        weights = (
            P(None, "dp", tensor),
            P(tensor, "dp"),
            P("dp", tensor),
            P(tensor, "dp"),
            P(tensor, "dp"),
            P(None, "dp"),
        )
        states = (
            P(None, None, "dp", tensor),
            P(None, tensor, "dp"),
            P(None, "dp", tensor),
            P(None, tensor, "dp"),
            P(None, tensor, "dp"),
            P(None, None, "dp"),
        )
        placed = jax.shard_map(
            layer_step,
            mesh=inner,
            in_specs=(rows, rows, P("dp")) + weights + states,
            out_specs=(rows, rows) + weights + weights + states,
            check_vma=False,
        )
        return placed(*args)

    return step
```

```python
import functools

import jax
import jax.numpy as jnp
from jax import lax
from jax.experimental import pallas as pl
from jax.experimental.pallas import tpu as pltpu
from jax.sharding import Mesh
from jax.sharding import PartitionSpec as P


L = 512
STEP = 10
HD = 64
LANES = 128
GRANT = 20 << 20


norm_eps = 1e-05
beta_one = 0.9
beta_two = 0.999
learn_rate = 0.02
decay_rate = 0.01
adam_eps = 1e-08
half = jnp.bfloat16
single = jnp.float32


def gelu_pair(before):
    cumul = 0.5 * (1.0 + lax.erf(before * 0.7071067811865476))
    density = jnp.exp(-0.5 * before * before) * 0.3989422804014327
    return (before * cumul, cumul + before * density)


def adamw_step(weight, moments, grad, decay):
    first_one = lax.broadcasted_iota(jnp.int32, moments.shape, 0) == 0
    state = jnp.where(
        first_one,
        beta_one * moments + (1.0 - beta_one) * grad,
        beta_two * moments + (1.0 - beta_two) * grad * grad,
    )
    first = beta_one * moments[0] + (1.0 - beta_one) * grad
    second = beta_two * moments[1] + (1.0 - beta_two) * grad * grad
    scale_one = 1.0 - beta_one**STEP
    scale_two = 1.0 - beta_two**STEP
    update = first / scale_one / (jnp.sqrt(second / scale_two) + adam_eps) + decay * weight
    return (weight - learn_rate * update, state)


def dot(a, b, dims, kind=single):
    return lax.dot_general(a, b, (dims, ((), ())), preferred_element_type=single).astype(kind)


def call(kernel, **options):
    params = pltpu.CompilerParams(vmem_limit_bytes=GRANT)
    return pl.pallas_call(kernel, compiler_params=params, **options)


NN = ((1,), (0,))
NT = ((1,), (1,))
TN = ((0,), (0,))


def attend_kernel(q_ref, k_ref, v_ref, mask_ref, out_ref, lse_ref):
    lane = lax.broadcasted_iota(jnp.int32, (1, LANES), 1)
    q, k, v = q_ref[...], k_ref[...], v_ref[...]
    out = lse = None
    for head in range(LANES // HD):
        mine = (lane >= head * HD) & (lane < (head + 1) * HD)
        q_h = jnp.where(mine, q, jnp.zeros_like(q))
        scores = dot(q_h, k, NT) * HD ** (-0.5) + mask_ref[...]
        row_max = jnp.max(scores, axis=-1, keepdims=True)
        exponent = jnp.exp(scores - row_max)
        total = jnp.sum(exponent, axis=-1, keepdims=True)
        prob = (exponent / total).astype(half)
        out_h = dot(prob, v, NN)
        lse_h = jnp.broadcast_to(row_max + jnp.log(total), out_h.shape)
        out = out_h if out is None else jnp.where(mine, out_h, out)
        lse = lse_h if lse is None else jnp.where(mine, lse_h, lse)
    out_ref[...] = out.astype(half)
    lse_ref[...] = lse


def group_block(j, per):
    return lambda i: (0, (i // per) * 4 * per + j * per + i % per)


def attend(projected, mask, per):
    rows, width = projected.shape
    blocks = width // (4 * LANES)
    block = (rows, LANES)
    return call(
        attend_kernel,
        grid=(blocks,),
        in_specs=[pl.BlockSpec(block, group_block(j, per)) for j in range(3)]
        + [pl.BlockSpec((1, rows), lambda i: (0, 0))],
        out_specs=[pl.BlockSpec(block, lambda i: (0, i))] * 2,
        out_shape=[
            jax.ShapeDtypeStruct((rows, width // 4), half),
            jax.ShapeDtypeStruct((rows, width // 4), single),
        ],
        cost_estimate=pl.CostEstimate(
            flops=blocks * 8 * rows * rows * LANES,
            bytes_accessed=rows * width * 4,
            transcendentals=blocks * 2 * rows * rows,
        ),
    )(projected, projected, projected, mask)


def attend_back_kernel(per, q_ref, k_ref, v_ref, up_ref, lse_ref, mask_ref, out_ref, sum_ref):
    block = pl.program_id(0)
    lane = lax.broadcasted_iota(jnp.int32, (1, LANES), 1)
    q, k, v, up = q_ref[...], k_ref[...], v_ref[...], up_ref[...]
    grads = None
    for head in range(LANES // HD):
        mine = (lane >= head * HD) & (lane < (head + 1) * HD)
        q_h = jnp.where(mine, q, jnp.zeros_like(q))
        up_h = jnp.where(mine, up, jnp.zeros_like(up))
        scores = dot(q_h, k, NT) * HD ** (-0.5) + mask_ref[...]
        prob = jnp.exp(scores - lse_ref[:, head * HD : head * HD + 1])
        d_prob = dot(up_h, v, NT)
        delta = jnp.sum(prob * d_prob, axis=-1, keepdims=True)
        d_score = (prob * (d_prob - delta) * HD ** (-0.5)).astype(half)
        now = (dot(d_score, k, NN), dot(d_score, q, TN), dot(prob.astype(half), up, TN))
        grads = now if grads is None else [jnp.where(mine, a, b) for a, b in zip(now, grads)]
    parts = [g.astype(half) for g in grads] + [jnp.zeros_like(q)]
    for j in range(4):
        start = ((block // per) * 4 * per + j * per + block % per) * LANES
        out_ref[:, pl.ds(pl.multiple_of(start, LANES), LANES)] = parts[j]
    row = lax.broadcasted_iota(jnp.int32, (8, LANES), 0)
    for j, grad in enumerate((grads[0], None, grads[2], None)):
        start = ((block // per) * 4 * per + j * per + block % per) * LANES
        total = 0.0 if grad is None else jnp.sum(grad, axis=0, keepdims=True)
        sums = jnp.where(row == 6, total, 0.0)
        sum_ref[:, pl.ds(pl.multiple_of(start, LANES), LANES)] = sums


def attend_back(projected, upstream, lse, mask, per):
    rows, width = projected.shape
    blocks = width // (4 * LANES)
    block = (rows, LANES)
    return call(
        functools.partial(attend_back_kernel, per),
        grid=(blocks,),
        in_specs=[pl.BlockSpec(block, group_block(j, per)) for j in range(3)]
        + [
            pl.BlockSpec(block, lambda i: (0, i)),
            pl.BlockSpec(block, lambda i: (0, i)),
            pl.BlockSpec((1, rows), lambda i: (0, 0)),
        ],
        out_specs=[
            pl.BlockSpec((rows, width), lambda i: (0, 0)),
            pl.BlockSpec((8, width), lambda i: (0, 0)),
        ],
        out_shape=[
            jax.ShapeDtypeStruct((rows, width), half),
            jax.ShapeDtypeStruct((8, width), single),
        ],
        cost_estimate=pl.CostEstimate(
            flops=blocks * 20 * rows * rows * LANES,
            bytes_accessed=rows * width * 6,
            transcendentals=blocks * 2 * rows * rows,
        ),
    )(projected, projected, projected, upstream, lse, mask)


def normal_rows(resid):
    center = resid - jnp.mean(resid, axis=-1, keepdims=True)
    inv_std = lax.rsqrt(jnp.mean(center * center, axis=-1, keepdims=True) + norm_eps)
    return center * inv_std, inv_std


def norm_back(scaled, normed, inv_std):
    return inv_std * (
        scaled
        - jnp.mean(scaled, axis=-1, keepdims=True)
        - normed * jnp.mean(scaled * normed, axis=-1, keepdims=True)
    )


def first_norm_kernel(x_ref, mine_ref, other_ref, vec_ref, hidden_ref, half_ref, normed_ref, inv_ref):
    attn = mine_ref[...].astype(single) + other_ref[...].astype(single)
    resid = x_ref[...].astype(single) + attn + vec_ref[0:1, :]
    normed, inv_std = normal_rows(resid)
    hidden = normed * (1.0 + vec_ref[1:2, :]) + vec_ref[2:3, :]
    hidden_ref[...] = hidden
    half_ref[...] = hidden.astype(half)
    normed_ref[...] = normed
    inv_ref[...] = jnp.broadcast_to(inv_std, inv_ref.shape)


def add_sums(sum_ref, start, terms):
    row = lax.broadcasted_iota(jnp.int32, sum_ref.shape, 0)
    now = jnp.zeros(sum_ref.shape, single)
    for i, term in enumerate(terms):
        total = jnp.sum(term, axis=0, keepdims=True)
        now = now + jnp.where(row == start + i, total, 0.0)

    @pl.when(pl.program_id(0) == 0)
    def _():
        sum_ref[...] = now

    @pl.when(pl.program_id(0) != 0)
    def _():
        sum_ref[...] += now


def second_norm_kernel(
    hidden_ref, mine_ref, other_ref, up_ref, live_ref, vec_ref, out_ref, two_ref, half_ref, sum_ref
):
    ffn = mine_ref[...].astype(single) + other_ref[...].astype(single)
    resid = hidden_ref[...] + ffn + vec_ref[3:4, :]
    normed, inv_std = normal_rows(resid)
    gain = 1.0 + vec_ref[4:5, :]
    out_ref[...] = (normed * gain + vec_ref[5:6, :]).astype(half)
    grad_out = jnp.where(live_ref[:, 0:1] > 0.0, up_ref[...].astype(single), 0.0)
    d_two = norm_back(grad_out * gain, normed, inv_std)
    two_ref[...] = d_two
    half_ref[...] = d_two.astype(half)
    add_sums(sum_ref, 3, [d_two, grad_out * normed, grad_out])


def first_back_kernel(
    two_ref, mine_ref, other_ref, normed_ref, inv_ref, vec_ref, one_ref, half_ref, sum_ref
):
    term = mine_ref[...].astype(single) + other_ref[...].astype(single)
    d_hidden = two_ref[...] + term
    normed = normed_ref[...]
    d_one = norm_back(d_hidden * (1.0 + vec_ref[1:2, :]), normed, inv_ref[:, 0:1])
    one_ref[...] = d_one
    half_ref[...] = d_one.astype(half)
    add_sums(sum_ref, 0, [d_one, d_hidden * normed, d_hidden])


def by_rows(kernel, inputs, outputs, sums):
    rows = inputs[0].shape[0]
    tile = min(rows, 128)

    def spec(shape):
        if shape[0] == rows:
            return pl.BlockSpec((tile, shape[1]), lambda i: (i, 0))
        return pl.BlockSpec(shape, lambda i: (0, 0))

    shapes = [jax.ShapeDtypeStruct((rows, w), kind) for w, kind in outputs]
    shapes += [jax.ShapeDtypeStruct((8, sums), single)] if sums else []
    return call(
        kernel,
        grid=(rows // tile,),
        in_specs=[spec(a.shape) for a in inputs],
        out_specs=[spec(a.shape) for a in shapes],
        out_shape=shapes,
        cost_estimate=pl.CostEstimate(
            flops=40 * rows * inputs[0].shape[1],
            bytes_accessed=20 * rows * inputs[0].shape[1],
            transcendentals=rows,
        ),
    )(*inputs)


def first_grad_kernel(
    size, per, x_ref, stack_ref, one_ref, heads_ref, vec_ref, qv_ref, unit_ref, out_ref
):
    out_ref[0:size, :] = dot(x_ref[...], stack_ref[...], TN, half)
    proj = dot(one_ref[...], heads_ref[...], TN, half)
    span = per * LANES
    for g in range(proj.shape[1] // span):
        start = (4 * g + 3) * span
        out_ref[0:size, start : start + span] = proj[:, g * span : (g + 1) * span]
    small = vec_ref[...] + qv_ref[...] + unit_ref[...]
    blank = jnp.zeros((out_ref.shape[0] - size - 8, small.shape[1]), single)
    out_ref[size:, :] = jnp.concatenate([small, blank], 0).astype(half)


def first_grad(x, stack, one, heads, vec, qv, unit, wanted, size, per, extra):
    rows, width = stack.shape
    first, stride = wanted[0], (wanted[1] - wanted[0] if len(wanted) > 1 else 1)
    assert wanted == [first + i * stride for i in range(len(wanted))]
    return call(
        functools.partial(first_grad_kernel, size, per),
        grid=(len(wanted),),
        in_specs=[
            pl.BlockSpec((rows, size), lambda i: (0, first + i * stride)),
            pl.BlockSpec(stack.shape, lambda i: (0, 0)),
            pl.BlockSpec((rows, size), lambda i: (0, first + i * stride)),
            pl.BlockSpec(heads.shape, lambda i: (0, 0)),
            pl.BlockSpec((8, width), lambda i: (0, first + i * stride)),
            whole_spec(qv.shape),
            whole_spec(unit.shape),
        ],
        out_specs=pl.BlockSpec((size + extra, width), lambda i: (i, 0)),
        out_shape=jax.ShapeDtypeStruct((len(wanted) * (size + extra), width), half),
        cost_estimate=pl.CostEstimate(
            flops=len(wanted) * 2 * rows * size * (width + heads.shape[1]),
            bytes_accessed=rows * width * 4,
            transcendentals=0,
        ),
    )(x, stack, one, heads, vec, qv, unit)


def flip(value, axis, bit):
    count = lax.axis_size(axis)
    return lax.ppermute(value, axis, [(i, i ^ bit) for i in range(count)])


def bits_of(count):
    return [1 << i for i in range(count.bit_length() - 1)]


def cut(value, start, size, axis):
    return lax.slice_in_dim(value, start, start + size, axis=axis)


class Pieces:
    def __init__(self, now, other, order, size, pitch, axis):
        held = [0]
        for bit in order[:-1]:
            held = held + [j ^ bit for j in held]
        self.arrays = (now, other)
        self.where = {}
        for i, j in enumerate(held):
            self.where[j] = (0, i * pitch)
            self.where[j ^ order[-1]] = (1, i * pitch)
        self.size, self.axis = size, axis

    def read(self, refs, j, columns=None):
        side, start = self.where[j]
        if self.axis == 1:
            return refs[side][:, start : start + self.size]
        if columns is None:
            return refs[side][start : start + self.size, :]
        return refs[side][start : start + self.size, columns]


def gather_dp(block, order, axis):
    now = block
    for step, bit in enumerate(order):
        other = flip(now, "dp", bit)
        if step + 1 < len(order):
            now = jnp.concatenate([now, other], axis)
    return now, other


def whole_spec(shape):
    return pl.BlockSpec(shape, lambda i: (0, 0))


def cost(flops, moved):
    return pl.CostEstimate(flops=flops, bytes_accessed=moved, transcendentals=0)


def project_kernel(weight, gelu, x_ref, now_ref, other_ref, row_ref, out_ref, *slope_ref):
    refs = (now_ref, other_ref)
    total = row_ref[...]
    for j in sorted(weight.where):
        x = x_ref[:, j * weight.size : (j + 1) * weight.size]
        total = total + dot(x, weight.read(refs, j), NN)
    if gelu:
        active, slope = gelu_pair(total)
        out_ref[...] = active.astype(half)
        slope_ref[0][...] = slope
    else:
        out_ref[...] = total.astype(half)


def project(x, weight, row, gelu):
    rows, width = x.shape[0], row.shape[0]
    tile = min(width, 256)
    column = lambda i: (0, i)
    shapes = [jax.ShapeDtypeStruct((rows, width), half)]
    if gelu:
        shapes.append(jax.ShapeDtypeStruct((rows, width), single))
    out = call(
        functools.partial(project_kernel, weight, gelu),
        grid=(width // tile,),
        in_specs=[whole_spec(x.shape)]
        + [pl.BlockSpec((a.shape[0], tile), column) for a in weight.arrays]
        + [pl.BlockSpec((1, tile), column)],
        out_specs=[pl.BlockSpec((rows, tile), column) for _ in shapes],
        out_shape=shapes,
        cost_estimate=cost(2 * rows * x.shape[1] * width, 4 * rows * width),
    )(x, *weight.arrays, row[None, :])
    return out if gelu else out[0]


def back_units_kernel(weight, up_ref, now_ref, other_ref, slope_ref, out_ref, sum_ref):
    refs = (now_ref, other_ref)
    total = 0.0
    for j in sorted(weight.where):
        up = up_ref[:, j * weight.size : (j + 1) * weight.size]
        total = total + dot(up, weight.read(refs, j), NT)
    d_pre = total * slope_ref[...]
    out_ref[...] = d_pre.astype(half)
    row = lax.broadcasted_iota(jnp.int32, sum_ref.shape, 0)
    sum_ref[...] = jnp.where(row == 7, jnp.sum(d_pre, axis=0, keepdims=True), 0.0)


def back_units(upstream, weight, slope):
    rows, width = slope.shape
    tile = min(width, 256)
    column = lambda i: (0, i)
    return call(
        functools.partial(back_units_kernel, weight),
        grid=(width // tile,),
        in_specs=[whole_spec(upstream.shape)]
        + [pl.BlockSpec((tile, a.shape[1]), lambda i: (i, 0)) for a in weight.arrays]
        + [pl.BlockSpec((rows, tile), column)],
        out_specs=[pl.BlockSpec((rows, tile), column), pl.BlockSpec((8, tile), column)],
        out_shape=[
            jax.ShapeDtypeStruct((rows, width), half),
            jax.ShapeDtypeStruct((8, width), single),
        ],
        cost_estimate=cost(2 * rows * upstream.shape[1] * width, 6 * rows * width),
    )(upstream, *weight.arrays, slope)


def blend_kernel(weights, columns, dims, *refs):
    out_ref = refs[-1]
    size = weights[0].size
    for j in sorted(weights[0].where):
        total = 0.0
        for c, weight in enumerate(weights):
            left, pair = refs[3 * c], refs[3 * c + 1 : 3 * c + 3]
            if columns is None:
                total = total + dot(left[...], weight.read(pair, j), dims)
                continue
            span = columns[0].stop - columns[0].start
            for g, window in enumerate(columns):
                part = left[:, g * span : (g + 1) * span]
                total = total + dot(part, weight.read(pair, j, window), dims)
        out_ref[:, j * size : (j + 1) * size] = total.astype(half)


def blend(lefts, weights, dims, columns=None):
    rows = lefts[0].shape[0]
    width = weights[0].size * len(weights[0].where)
    tile = min(rows, 256)
    inputs, specs = [], []
    for left, weight in zip(lefts, weights):
        inputs += [left, *weight.arrays]
        specs.append(pl.BlockSpec((tile, left.shape[1]), lambda i: (i, 0)))
        specs += [whole_spec(a.shape) for a in weight.arrays]
    return call(
        functools.partial(blend_kernel, weights, columns, dims),
        grid=(rows // tile,),
        in_specs=specs,
        out_specs=pl.BlockSpec((tile, width), lambda i: (i, 0)),
        out_shape=jax.ShapeDtypeStruct((rows, width), half),
        cost_estimate=cost(4 * rows * width * lefts[0].shape[1], 8 * rows * width),
    )(*inputs)


def back_heads_kernel(weight, columns, up_ref, now_ref, other_ref, out_ref):
    refs = (now_ref, other_ref)
    span = columns[0].stop - columns[0].start
    for g, window in enumerate(columns):
        total = 0.0
        for j in sorted(weight.where):
            up = up_ref[:, j * weight.size : (j + 1) * weight.size]
            total = total + dot(up, weight.read(refs, j, window), NN)
        out_ref[:, g * span : (g + 1) * span] = total.astype(half)


def back_heads(upstream, weight, columns):
    rows = upstream.shape[0]
    width = sum(w.stop - w.start for w in columns)
    return call(
        functools.partial(back_heads_kernel, weight, columns),
        grid=(1,),
        in_specs=[whole_spec(a.shape) for a in (upstream, *weight.arrays)],
        out_specs=whole_spec((rows, width)),
        out_shape=jax.ShapeDtypeStruct((rows, width), half),
        cost_estimate=cost(2 * rows * upstream.shape[1] * width, 8 * rows * width),
    )(upstream, *weight.arrays)


def block_grad_kernel(left_ref, right_ref, out_ref):
    out_ref[...] = dot(left_ref[...], right_ref[...], TN, half)


def block_grad(left, right, wanted, size, rows_cut):
    count = len(wanted)
    first, stride = wanted[0], (wanted[1] - wanted[0] if count > 1 else 1)
    assert wanted == [first + i * stride for i in range(count)]
    rows = left.shape[0]
    chosen = pl.BlockSpec((rows, size), lambda i: (0, first + i * stride))
    if rows_cut:
        specs = [chosen, whole_spec(right.shape)]
        block, index = (size, right.shape[1]), lambda i: (i, 0)
        shape = (count * size, right.shape[1])
    else:
        specs = [whole_spec(left.shape), chosen]
        block, index = (left.shape[1], size), lambda i: (0, i)
        shape = (left.shape[1], count * size)
    return call(
        block_grad_kernel,
        grid=(count,),
        in_specs=specs,
        out_specs=pl.BlockSpec(block, index),
        out_shape=jax.ShapeDtypeStruct(shape, half),
        cost_estimate=cost(2 * rows * shape[0] * shape[1], 4 * shape[0] * shape[1]),
    )(left, right)


def halves(members, bit):
    return [j for j in members if j & bit], [j for j in members if not j & bit]


def scatter_dp(away, stay, order, axis):
    held = list(range(lax.axis_size("dp")))
    for step, bit in enumerate(order):
        other = flip(away, "dp", bit)
        held = halves(held, bit)[1]
        if step + 1 == len(order):
            return (stay.astype(single) + other.astype(single)).astype(half)
        size = stay.shape[axis] // len(held)

        def pick(value, wanted):
            parts = [cut(value, held.index(j) * size, size, axis) for j in wanted]
            return parts[0] if len(parts) == 1 else jnp.concatenate(parts, axis)

        def added(wanted):
            total = pick(stay, wanted).astype(single) + pick(other, wanted).astype(single)
            return total.astype(half)

        away, stay = (added(part) for part in halves(held, order[step + 1]))


def gather_z(shard, axis):
    bits = bits_of(lax.axis_size("z"))
    now = shard
    for bit in bits[:-1]:
        now = jnp.concatenate([now, flip(now, "z", bit)], axis)
    return now, flip(now, "z", bits[-1])


def scatter_z(colors, axis):
    bits = bits_of(lax.axis_size("z"))
    held = list(range(1 << len(bits)))
    size = colors[0].shape[axis] * 2 // len(held)
    slots = [cut(color, i * size, size, axis) for color in colors for i in range(len(held) // 2)]
    for bit in bits:
        leave, stay = halves(held, bit)
        parts = [[slots[held.index(r)] for r in group] for group in (leave, stay)]
        away, keep = (p[0] if len(p) == 1 else jnp.concatenate(p, axis) for p in parts)
        other = flip(away, "z", bit)
        if bit == bits[-1]:
            return keep, other
        total = (keep.astype(single) + other.astype(single)).astype(half)
        held = stay
        slots = [cut(total, i * size, size, axis) for i in range(len(held))]


def added(pair):
    return pair[0].astype(single) + pair[1].astype(single)


def first_update_kernel(
    keep_ref, other_ref, qkv_ref, qkv_m_ref, proj_ref, proj_m_ref,
    sum_ref, proj_sum_ref, new_ref, proj_new_ref, state_ref, proj_state_ref, small_ref,
):
    size, width = qkv_ref.shape[1:]
    grad = keep_ref[...].astype(single) + other_ref[...].astype(single)
    small_ref[...] = grad[size:]

    def step(weight, first, second, total):
        first = beta_one * first + (1.0 - beta_one) * total
        second = beta_two * second + (1.0 - beta_two) * total * total
        scale_one = 1.0 - beta_one**STEP
        scale_two = 1.0 - beta_two**STEP
        update = first / scale_one / (jnp.sqrt(second / scale_two) + adam_eps)
        return weight - learn_rate * (update + decay_rate * weight), first, second

    for j in range(3):
        total = grad[:size, j * width : (j + 1) * width]
        sum_ref[j] = total
        new, first, second = step(qkv_ref[j], qkv_m_ref[0, j], qkv_m_ref[1, j], total)
        new_ref[j] = new
        state_ref[0, j] = first
        state_ref[1, j] = second
    total = grad[:size, 3 * width :].T
    proj_sum_ref[...] = total
    new, first, second = step(proj_ref[...], proj_m_ref[0], proj_m_ref[1], total)
    proj_new_ref[...] = new
    proj_state_ref[0] = first
    proj_state_ref[1] = second


def first_update(pair, qkv, qkv_m, proj, proj_m):
    extra = pair[0].shape[0] - qkv.shape[1]
    shapes = [a.shape for a in (qkv, proj, qkv, proj, qkv_m, proj_m)]
    shapes.append((extra, pair[0].shape[1]))
    operands = (*pair, qkv, qkv_m, proj, proj_m)

    def full(shape):
        return pl.BlockSpec(shape, lambda i: (0,) * len(shape))

    return call(
        first_update_kernel,
        grid=(1,),
        in_specs=[full(a.shape) for a in operands],
        out_specs=[full(shape) for shape in shapes],
        out_shape=[jax.ShapeDtypeStruct(shape, single) for shape in shapes],
        cost_estimate=cost(20 * qkv.size, 40 * qkv.size),
    )(*operands)


def sum_members(term):
    now = term
    bits = bits_of(lax.axis_size("g"))
    for bit in bits:
        other = flip(now, "g", bit)
        if bit != bits[-1]:
            now = (now.astype(single) + other.astype(single)).astype(half)
    return now, other


def gather_members(rows):
    me = lax.axis_index("g")
    for bit in bits_of(lax.axis_size("g")):
        other = flip(rows, "g", bit)
        rows = jnp.where(
            (me & bit) != 0,
            jnp.concatenate([other, rows], 0),
            jnp.concatenate([rows, other], 0),
        )
    return rows


def scatter_members(term):
    me = lax.axis_index("g")
    now = term.astype(half)
    for bit in reversed(bits_of(lax.axis_size("g"))):
        size = now.shape[0] // 2
        side = ((me & bit) != 0).astype(jnp.int32)
        send = lax.dynamic_slice_in_dim(now, (1 - side) * size, size, 0)
        keep = lax.dynamic_slice_in_dim(now, side * size, size, 0)
        total = keep.astype(single) + flip(send, "g", bit).astype(single)
        now = total.astype(half)
    return total


def reorder(matrix, count, member):
    size = matrix.shape[-1] // count
    return jnp.concatenate(
        [
            lax.dynamic_slice_in_dim(matrix, (member ^ j) * size, size, matrix.ndim - 1)
            for j in range(count)
        ],
        -1,
    )


def layer_step(
    block_in,
    cotangent,
    lengths,
    qkv_weight,
    proj_weight,
    expand_weight,
    reduce_weight,
    split_bias,
    vector_params,
    qkv_moments,
    proj_moments,
    expand_moments,
    reduce_moments,
    bias_moments,
    vector_moments,
):
    n_dp, n_z = lax.axis_size("dp"), lax.axis_size("z")
    dp, z, member = lax.axis_index("dp"), lax.axis_index("z"), lax.axis_index("g")
    share = block_in.shape[0]
    model = block_in.shape[1]
    width = qkv_weight.shape[2]
    part = model // n_dp
    heads = split_bias.shape[0]
    bias_part = split_bias.shape[1]
    pair = n_z // 2
    ganged = 1 if width % LANES == 0 else pair
    gang = ganged * width
    per = gang // LANES
    up = bits_of(n_dp)
    down = up[::-1]
    order_q, order_e, order_r = (up, up), (down, up), (down, up)
    extra = -(-max(6 + heads, 8) // 16) * 16

    def wide(rows, count):
        return jnp.pad(rows, ((0, 0), (0, count - rows.shape[1])))

    small = jnp.concatenate(
        [
            wide(vector_params.astype(half), 4 * width),
            wide(split_bias.astype(half), 4 * width),
            jnp.zeros((extra - 6 - heads, 4 * width), half),
        ],
        0,
    )
    own_q = jnp.concatenate(
        [qkv_weight[j].astype(half) for j in range(3)] + [proj_weight.astype(half).T], 1
    )
    own_q = jnp.concatenate([own_q, small], 0)
    own_e = expand_weight.astype(half)
    own_r = reduce_weight.astype(half)

    weight_q, weight_e, weight_r, small_q = [], [], [], []

    def ganged_columns(matrix):
        if ganged == 1:
            return matrix
        cut_up = matrix.reshape(matrix.shape[0], -1, ganged, 4, width)
        return cut_up.transpose(0, 1, 3, 2, 4).reshape(matrix.shape)

    for c, block in enumerate(gather_z(own_q, 1)):
        arrays = gather_dp(block, order_q[c], 0)
        held = Pieces(*arrays, order_q[c], extra, part + extra, 0)
        small_q.append(
            [
                cut(arrays[held.where[j][0]], held.where[j][1] + part, extra, 0)
                for j in range(n_dp)
            ]
        )
        arrays = [ganged_columns(a) for a in arrays]
        weight_q.append(Pieces(*arrays, order_q[c], part, part + extra, 0))
    for c, block in enumerate(gather_z(own_e, 1)):
        arrays = gather_dp(block, order_e[c], 0)
        weight_e.append(Pieces(*arrays, order_e[c], part, part, 0))
    for c, block in enumerate(gather_z(own_r, 0)):
        if c == 0:
            arrays = gather_dp(block, order_r[c], 1)
            weight_r.append(Pieces(*arrays, order_r[c], part, part, 1))
            continue
        tall = block.shape[0] // 2
        blocks = []
        for n, order in enumerate((up, down)):
            arrays = gather_dp(cut(block, n * tall, tall, 0), order, 1)
            held = Pieces(*arrays, order, part, part, 1)
            blocks.append(
                [cut(arrays[held.where[j][0]], held.where[j][1], part, 1) for j in range(n_dp)]
            )
        sides = [
            jnp.concatenate([jnp.concatenate([b[j] for j in js], 1) for b in blocks], 0)
            for js in (range(n_dp // 2), range(n_dp // 2, n_dp))
        ]
        weight_r.append(Pieces(*sides, up, part, part, 1))

    vectors = jnp.concatenate([small_q[0][j][:6, :part] for j in range(n_dp)], 1)
    vectors = jnp.pad(vectors.astype(single), ((0, 2), (0, 0)))
    mine_at = jnp.arange(n_dp, dtype=jnp.int32)
    picked = ((mine_at[:, None] ^ dp) == mine_at[None, :]).astype(half)

    def biases_of(small_rows):
        rel = jnp.stack([p[6 : 6 + heads] for p in small_rows])
        rel = rel.reshape(n_dp, heads, pair, 4 * width)[..., :bias_part]
        rows = dot(picked, rel.reshape(n_dp, -1), NN).reshape(n_dp, heads, pair, bias_part)
        return rows.transpose(2, 1, 0, 3).reshape(pair, heads, -1)

    length = lax.dynamic_index_in_dim(lengths, z, 0, keepdims=False)
    live = jnp.arange(L, dtype=jnp.int32) < length
    mask = jnp.where(live, 0.0, -jnp.inf).astype(single)[None, :]
    live_rows = jnp.broadcast_to(live[:, None].astype(single), (L, LANES))

    x_full = gather_members(reorder(block_in, n_dp, dp))
    up_full = gather_members(reorder(cotangent, n_dp, dp))

    projected, heads_out, lse, bias_rows = [], [], [], []
    groups = pair // ganged
    out_columns = [slice((4 * i + 3) * gang, (4 * i + 4) * gang) for i in range(groups)]
    for c in range(2):
        if c:
            small_q[c], projected[0] = lax.optimization_barrier((small_q[c], projected[0]))
        bias_rows.append(biases_of(small_q[c]))
        rows = bias_rows[c].reshape(groups, ganged, heads, -1)
        q_bias = rows[..., :HD].reshape(groups, gang)
        v_bias = rows[..., HD : 2 * HD].reshape(groups, gang)
        nothing = jnp.zeros_like(q_bias)
        row = jnp.concatenate([q_bias, nothing, v_bias, nothing], 1).reshape(-1)
        projected.append(project(x_full, weight_q[c], row, False))
        out, log_total = attend(projected[c], mask, per)
        heads_out.append(out)
        lse.append(log_total)
    attn_term = blend(heads_out, weight_q, NT, out_columns)
    mine, other = sum_members(attn_term)
    hidden_f, hidden_b, normed_one, inv_one = by_rows(
        first_norm_kernel,
        (x_full, mine, other, vectors),
        ((model, single), (model, half), (model, single), (LANES, single)),
        0,
    )
    active_b, slopes = [], []
    for c in range(2):
        row = bias_rows[c][..., 2 * HD :].reshape(-1)
        active, slope = project(hidden_b, weight_e[c], row, True)
        active_b.append(active)
        slopes.append(slope)
    ffn_term = blend(active_b, weight_r, NN)
    mine, other = sum_members(ffn_term)
    out_b, d_two, d_two_b, sums_two = by_rows(
        second_norm_kernel,
        (hidden_f, mine, other, up_full, live_rows, vectors),
        ((model, half), (model, single), (model, half)),
        model,
    )

    members = list(range(n_dp))
    firsts = (down[0], up[0])
    back = (down, up)
    got_r, got_e, got_q = [], [], []
    sent_r = []
    for c in range(2):
        sent_r.append(block_grad(active_b[c], d_two_b, halves(members, firsts[c])[0], part, False))
    for c in range(2):
        kept = block_grad(active_b[c], d_two_b, halves(members, firsts[c])[1], part, False)
        got_r.append(scatter_dp(sent_r[c], kept, back[c], 1))
    unit_sums, d_pre_b = [], []
    for c in range(2):
        d_pre, sums = back_units(d_two_b, weight_r[c], slopes[c])
        unit_sums.append(sums)
        d_pre_b.append(d_pre)
    hidden_term = blend(d_pre_b, weight_e, NT)
    for c in range(2):
        leave, kept = halves(members, firsts[c])
        leave = block_grad(hidden_b, d_pre_b[c], leave, part, True)
        kept = block_grad(hidden_b, d_pre_b[c], kept, part, True)
        got_e.append(scatter_dp(leave, kept, back[c], 0))
    mine, other = sum_members(hidden_term)
    d_one, d_one_b, sums_one = by_rows(
        first_back_kernel,
        (d_two, mine, other, normed_one, inv_one, vectors),
        ((model, single), (model, half)),
        model,
    )
    vec = (sums_one + sums_two).reshape(8, n_dp, 1, part)
    vec = jnp.pad(vec, ((0, 0), (0, 0), (0, 0), (0, 4 * width - part)))
    vec = jnp.broadcast_to(vec, (8, n_dp, pair, 4 * width)).reshape(8, -1)
    vec = ganged_columns(vec)
    stacks = []
    for c in range(2):
        d_heads = back_heads(d_one_b, weight_q[c], out_columns)
        d_stack, sums = attend_back(projected[c], d_heads, lse[c], mask, per)
        stacks.append(d_stack)
        unit = ganged_columns(unit_sums[c])
        leave, kept = halves(members, firsts[c])
        operands = (x_full, d_stack, d_one_b, heads_out[c], vec, sums, unit)
        leave = first_grad(*operands, leave, part, per, extra)
        kept = first_grad(*operands, kept, part, per, extra)
        got_q.append(scatter_dp(leave, kept, back[c], 0))
    if ganged > 1:
        got_q = [
            g.reshape(part + extra, -1, 4, ganged, width)
            .transpose(0, 1, 3, 2, 4)
            .reshape(part + extra, -1)
            for g in got_q
        ]

    reduce_sum = added(scatter_z(got_r, 0))
    expand_sum = added(scatter_z(got_e, 1))
    qkv_sum, proj_sum, qkv_new, proj_new, qkv_state, proj_state, packed = first_update(
        scatter_z(got_q, 1), qkv_weight, qkv_moments, proj_weight, proj_moments
    )
    vector_sum = packed[:6, :part]
    bias_all = jnp.concatenate(
        [
            packed[6, :width].reshape(heads, HD),
            packed[6, 2 * width : 3 * width].reshape(heads, HD),
            packed[7].reshape(heads, -1),
        ],
        1,
    )
    bias_sum = lax.dynamic_slice_in_dim(bias_all, dp * bias_part, bias_part, 1)

    out_b, stacks = lax.optimization_barrier((out_b, stacks))
    input_term = blend(stacks, weight_q, NT)
    first_row = member * share
    block_out = reorder(lax.dynamic_slice_in_dim(out_b, first_row, share, 0), n_dp, dp)
    own_one = lax.dynamic_slice_in_dim(d_one, first_row, share, 0)
    input_grad = reorder((own_one + scatter_members(input_term)).astype(half), n_dp, dp)

    expand_new, expand_state = adamw_step(expand_weight, expand_moments, expand_sum, decay_rate)
    reduce_new, reduce_state = adamw_step(reduce_weight, reduce_moments, reduce_sum, decay_rate)
    bias_new, bias_state = adamw_step(split_bias, bias_moments, bias_sum, 0.0)
    vector_new, vector_state = adamw_step(vector_params, vector_moments, vector_sum, 0.0)
    return (
        block_out,
        input_grad,
        qkv_sum,
        proj_sum,
        expand_sum,
        reduce_sum,
        bias_sum,
        vector_sum,
        qkv_new,
        proj_new,
        expand_new,
        reduce_new,
        bias_new,
        vector_new,
        qkv_state,
        proj_state,
        expand_state,
        reduce_state,
        bias_state,
        vector_state,
    )


def solution(mesh):
    n_dp, n_tensor = mesh.devices.shape

    def step(*args):
        share = args[0].shape[0] // (n_dp * n_tensor)
        members = L // share
        inner = Mesh(
            mesh.devices.reshape(n_dp, n_tensor // members, members), ("dp", "z", "g")
        )
        tensor = ("z", "g")
        rows = P(("dp", "z", "g"), None)
        weights = (
            P(None, "dp", tensor),
            P(tensor, "dp"),
            P("dp", tensor),
            P(tensor, "dp"),
            P(tensor, "dp"),
            P(None, "dp"),
        )
        states = (
            P(None, None, "dp", tensor),
            P(None, tensor, "dp"),
            P(None, "dp", tensor),
            P(None, tensor, "dp"),
            P(None, tensor, "dp"),
            P(None, None, "dp"),
        )
        placed = jax.shard_map(
            layer_step,
            mesh=inner,
            in_specs=(rows, rows, P("dp")) + weights + states,
            out_specs=(rows, rows) + weights + weights + states,
            check_vma=False,
        )
        return placed(*args)

    return step
```
